256 devices in a mesh: view: 32 (over z, y), head: 8 (over x, core).
Axes of the slice: x: 4, y: 4, z: 8, core: 2. Of those that a mesh axis runs over, the one named last changes fastest.
Arguments:
- query_rows: bfloat16 [32768, 1024], P('view', 'head'), may hold values from -20 to 20
- key_rows: bfloat16 [32768, 1024], P('view', 'head'), may hold values from -6 to 6
- value_rows: bfloat16 [32768, 1024], P('view', 'head'), may hold values from -12 to 12
- out_weight: bfloat16 [1024, 1024], replicated, may hold values from -0.1875 to 0.1875
- out_grad: bfloat16 [32768, 1024], P('view', 'head'), may hold values from -12 to 12
- source_view: int32 [32, 16], replicated, may hold values from 0 to 31, as said below
- source_block: int32 [32, 16], replicated, may hold values from 0 to 7
Outputs:
- mixed_out: bfloat16 [32768, 1024], P('view', 'head')
- query_grad: bfloat16 [32768, 1024], P('view', 'head')
- key_grad: bfloat16 [32768, 1024], P('view', 'head')
- value_grad: bfloat16 [32768, 1024], P('view', 'head')
The draws below stay inside these ranges and needn't reach their ends.
Inputs may be any that keep to these rules, and one draw needn't show every extreme that they name: `source_view`: for each query view the 16 slots name distinct pairs of source view and block. No source view is named by more than 1 slots of one query view, and for every query view some source view is named by exactly 1 of its slots.
All inputs are finite; a program needn't handle non-finite values.
Results may differ from the reference program's by a relative error of at most 0.014.
Values may be sent and summed in bfloat16 or wider, within the bound.
A program may use at most 128 MiB of HBM per device.

```python
import jax
import jax.numpy as jnp
from jax import lax

D = 1024
HEADS = 16
HEAD_DIM = 64
BLOCK_TOKENS = 128
SLOTS_PER_QUERY = 16
VIEW_TOK = 1024
TOTAL_VIEWS = 32
KEYS = 2048
CAP = 1


def routing(key):
    block_count = VIEW_TOK // BLOCK_TOKENS
    unit_count = TOTAL_VIEWS * CAP
    unit_source = jnp.arange(unit_count, dtype=jnp.int32) // CAP
    popular = jax.random.randint(jax.random.fold_in(key, 11), (TOTAL_VIEWS,), 0, 4)
    forced = jax.random.randint(jax.random.fold_in(key, 12), (TOTAL_VIEWS,), 0, TOTAL_VIEWS)
    jitter = jax.random.randint(jax.random.fold_in(key, 13), (TOTAL_VIEWS, unit_count), 0, 4096)
    block_ranking = jitter + 2048 * popular[unit_source][None, :] + (1 << 20) * (unit_source[None, :] == forced[:, None]).astype(jnp.int32)
    block_ranking = block_ranking * unit_count + jnp.arange(unit_count, dtype=jnp.int32)[None, :]
    selected_blocks = jnp.argsort(-block_ranking, axis=1)[:, :SLOTS_PER_QUERY].astype(jnp.int32)
    source = selected_blocks // CAP
    copies = selected_blocks % CAP
    shuffle = jax.random.randint(jax.random.fold_in(key, 14), (TOTAL_VIEWS, TOTAL_VIEWS, block_count), 0, 1 << 16)
    shuffle = shuffle * block_count + jnp.arange(block_count, dtype=jnp.int32)[None, None, :]
    perms = jnp.argsort(shuffle, axis=-1).astype(jnp.int32)
    per_view = perms[jnp.arange(TOTAL_VIEWS, dtype=jnp.int32)[:, None], source]
    blocks = jnp.take_along_axis(per_view, copies[:, :, None], axis=2)[:, :, 0]
    return (source.astype(jnp.int32), blocks.astype(jnp.int32))


def draw_source_view(key, part):
    return routing(key)[0]


def draw_source_block(key, part):
    return routing(key)[1]


def draw_query_rows(key, part):
    row_count = TOTAL_VIEWS * VIEW_TOK
    result = 2.0 * jax.random.truncated_normal(jax.random.fold_in(key, 35), -6.0, 6.0, (row_count, D))
    return result.astype(jnp.bfloat16)


def draw_key_rows(key, part):
    row_count = TOTAL_VIEWS * VIEW_TOK
    result = jax.random.truncated_normal(jax.random.fold_in(key, 43), -6.0, 6.0, (row_count, D))
    return result.astype(jnp.bfloat16)


def steps_of(key, dims, shards, least, top_value):
    loudness = 1.0
    for dim, shards_of in shards:
        draws = jax.random.uniform(jax.random.fold_in(jax.random.fold_in(key, 6), dim), (shards_of,), jnp.float32, least / len(shards), top_value / len(shards))
        loudness = loudness * jnp.repeat(jnp.exp(draws), dims[dim] // shards_of).reshape((-1,) + (1,) * (len(dims) - 1 - dim))
    return loudness


def normal_values(rng, extent, spread, most, split=(), kind=jnp.bfloat16):
    loudness = steps_of(rng, extent, split, -0.22, 0.18) if split else 1.0
    entries = jax.random.normal(rng, extent, jnp.float32) * spread * loudness
    return jnp.minimum(jnp.maximum(entries, -most), most).astype(kind)


def setup_inputs(seed: int = 0) -> dict:
    splits = jax.random.split(jax.random.key(seed), 8)
    query_rows = draw_query_rows(jax.random.fold_in(splits[7], 71), 0)
    key_rows = draw_key_rows(jax.random.fold_in(splits[7], 71), 0)
    value_rows = normal_values(splits[2], (TOTAL_VIEWS * VIEW_TOK, D), 2.0, 12.0, ((0, 32), (1, 8)))
    out_weight = normal_values(splits[3], (D, D), D ** -0.5, 0.1875)
    out_grad = normal_values(splits[4], (TOTAL_VIEWS * VIEW_TOK, D), 2.0, 12.0, ((0, 32), (1, 8)))
    source_view = draw_source_view(jax.random.fold_in(splits[7], 71), 0)
    source_block = draw_source_block(jax.random.fold_in(splits[7], 71), 0)
    return dict(query_rows=query_rows, key_rows=key_rows, value_rows=value_rows, out_weight=out_weight, out_grad=out_grad, source_view=source_view, source_block=source_block)


def reference(query_rows, key_rows, value_rows, out_weight, out_grad, source_view, source_block):
    score_scale = HEAD_DIM ** -0.5
    leading_rows = source_view * VIEW_TOK + source_block * BLOCK_TOKENS
    block_passes = jnp.arange(BLOCK_TOKENS, dtype=jnp.int32)
    needed_blocks = (leading_rows[:, :, None] + block_passes[None, None, :]).reshape(TOTAL_VIEWS, SLOTS_PER_QUERY * BLOCK_TOKENS).astype(jnp.int32)
    query_views = query_rows.reshape(TOTAL_VIEWS, VIEW_TOK, D)
    grad_views = out_grad.reshape(TOTAL_VIEWS, VIEW_TOK, D)

    def one_view(totals, inputs):
        grad_keys, grad_values = totals
        query_view, grad_view, index = inputs
        key_heads = jnp.take(key_rows, index, axis=0).reshape(KEYS, HEADS, HEAD_DIM).astype(jnp.float32)
        value_heads = jnp.take(value_rows, index, axis=0).reshape(KEYS, HEADS, HEAD_DIM).astype(jnp.float32)
        query_heads = query_view.reshape(VIEW_TOK, HEADS, HEAD_DIM).astype(jnp.float32)
        scores = jnp.einsum("qhd,khd->hqk", query_heads, key_heads) * score_scale
        row_top = jnp.max(scores, axis=-1, keepdims=True)
        shifted = jnp.exp(scores - row_top)
        probability = shifted / jnp.sum(shifted, axis=-1, keepdims=True)
        weights = lax.optimization_barrier(probability.astype(jnp.bfloat16))
        attended = jnp.einsum("hqk,khd->qhd", weights.astype(jnp.float32), value_heads)
        attended = lax.optimization_barrier(attended.reshape(VIEW_TOK, D).astype(jnp.bfloat16))
        mixed = jnp.dot(attended, out_weight, preferred_element_type=jnp.float32).astype(jnp.bfloat16)
        attended_grad = jnp.dot(grad_view, out_weight.T, preferred_element_type=jnp.float32)
        attended_grad = lax.optimization_barrier(attended_grad.astype(jnp.bfloat16))
        grad_heads = attended_grad.reshape(VIEW_TOK, HEADS, HEAD_DIM).astype(jnp.float32)
        out_heads = attended.reshape(VIEW_TOK, HEADS, HEAD_DIM).astype(jnp.float32)
        grad_prob = jnp.einsum("qhd,khd->hqk", grad_heads, value_heads)
        row_delta = jnp.einsum("qhd,qhd->hq", out_heads, grad_heads)[:, :, None]
        grad_scores = lax.optimization_barrier((probability * (grad_prob - row_delta)).astype(jnp.bfloat16))
        grad_scores = grad_scores.astype(jnp.float32)
        query_grad = jnp.einsum("hqk,khd->qhd", grad_scores, key_heads) * score_scale
        query_grad = query_grad.reshape(VIEW_TOK, D).astype(jnp.bfloat16)
        key_part = (jnp.einsum("hqk,qhd->khd", grad_scores, query_heads) * score_scale).reshape(KEYS, D)
        value_part = jnp.einsum("hqk,qhd->khd", weights.astype(jnp.float32), grad_heads).reshape(KEYS, D)
        grad_keys = grad_keys.at[index].add(key_part)
        grad_values = grad_values.at[index].add(value_part)
        return (grad_keys, grad_values), (mixed, query_grad)

    zero_rows = jnp.zeros((TOTAL_VIEWS * VIEW_TOK, D), jnp.float32)
    (grad_keys, grad_values), (mixed, query_grad) = lax.scan(one_view, (zero_rows, zero_rows), (query_views, grad_views, needed_blocks))
    mixed_out = mixed.reshape(TOTAL_VIEWS * VIEW_TOK, D)
    query_grad = query_grad.reshape(TOTAL_VIEWS * VIEW_TOK, D)
    return mixed_out, query_grad, grad_keys.astype(jnp.bfloat16), grad_values.astype(jnp.bfloat16)
```

```python
import functools

import jax
import jax.numpy as jnp
from jax import lax
from jax.experimental import pallas as pl
from jax.experimental.pallas import tpu as pltpu
from jax.sharding import PartitionSpec as P

HEAD_DIM = 64
BLOCK = 128
SCALE = HEAD_DIM ** -0.5
LOG2E = 1.4426950408889634
QB = 256
KC = 256


def dot(a, b):
    return jnp.dot(a, b, preferred_element_type=jnp.float32)


def attention_kernel(
    idx, q_ref, rk_ref, rv_ref, da_ref,
    att_ref, dq_ref, dk_ref, dv_ref,
    k_s, v_s, kt_s, vt_s, s_s, p_s, dk_a, dv_a,
):
    slots = idx.shape[0]
    keys = slots * BLOCK
    tokens = q_ref.shape[0]
    for j in range(slots):
        rows = pl.ds(j * BLOCK, BLOCK)
        kb = rk_ref[idx[j]]
        vb = rv_ref[idx[j]]
        k_s[rows, :] = kb
        v_s[rows, :] = vb
        kt_s[:, rows] = kb.T
        vt_s[:, rows] = vb.T
    dk_a[...] = jnp.zeros_like(dk_a)
    dv_a[...] = jnp.zeros_like(dv_a)
    chunks = keys // KC
    lane = lax.broadcasted_iota(jnp.int32, (QB, 2 * HEAD_DIM), 1)

    def step(i, carry):
        qrows = pl.ds(pl.multiple_of(i * QB, QB), QB)
        q = q_ref[qrows, :]
        da = da_ref[qrows, :]
        qt = q.T
        dat = da.T
        atts = []
        dqs = []
        for h in range(2):
            hd = slice(h * HEAD_DIM, (h + 1) * HEAD_DIM)
            mine = (lane // HEAD_DIM) == h
            qh = jnp.where(mine, q, jnp.zeros_like(q))
            dah = jnp.where(mine, da, jnp.zeros_like(da))
            qth = qt[hd, :]
            dath = dat[hd, :]
            top = None
            for c in range(chunks):
                rows = pl.ds(c * KC, KC)
                s = dot(k_s[rows, hd], qth)
                s_s[rows, :] = s
                m = jnp.max(s, axis=0, keepdims=True)
                top = m if top is None else jnp.maximum(top, m)
            shift = top * (SCALE * LOG2E)
            total = jnp.zeros((1, QB), jnp.float32)
            for c in range(chunks):
                rows = pl.ds(c * KC, KC)
                e = jnp.exp2(s_s[rows, :] * (SCALE * LOG2E) - shift)
                s_s[rows, :] = e
                total = total + jnp.sum(e, axis=0, keepdims=True)
            inv = 1.0 / total
            for c in range(chunks):
                rows = pl.ds(c * KC, KC)
                p = s_s[rows, :] * inv
                pb = p.astype(jnp.bfloat16)
                p_s[rows, :] = pb
                dv_a[rows, :] += dot(pb, dah)
            att = dot(vt_s[hd, :], p_s[...]).astype(jnp.bfloat16)
            atts.append(att)
            delta = jnp.sum(
                att.astype(jnp.float32) * dath.astype(jnp.float32), axis=0, keepdims=True
            )
            for c in range(chunks):
                rows = pl.ds(c * KC, KC)
                dp = dot(v_s[rows, hd], dath)
                ds = ((s_s[rows, :] * inv) * (dp - delta)).astype(jnp.bfloat16)
                p_s[rows, :] = ds
                dk_a[rows, :] += dot(ds, qh)
            dqs.append(dot(kt_s[hd, :], p_s[...]) * SCALE)
        att_ref[qrows, :] = jnp.concatenate(atts, axis=0).T
        dq_ref[qrows, :] = jnp.concatenate(dqs, axis=0).astype(jnp.bfloat16).T
        return carry

    lax.fori_loop(0, tokens // QB, step, 0)
    for j in range(slots):
        rows = pl.ds(j * BLOCK, BLOCK)
        dk_ref[idx[j]] = (dk_a[rows, :] * SCALE).astype(jnp.bfloat16)
        dv_ref[idx[j]] = dv_a[rows, :].astype(jnp.bfloat16)


def attention(idx, q, rk, rv, da):
    tokens, columns = q.shape
    keys = idx.shape[0] * BLOCK
    vm = pl.BlockSpec(memory_space=pltpu.VMEM)
    bf, f32 = jnp.bfloat16, jnp.float32
    return pl.pallas_call(
        attention_kernel,
        out_shape=(
            jax.ShapeDtypeStruct((tokens, columns), bf),
            jax.ShapeDtypeStruct((tokens, columns), bf),
            jax.ShapeDtypeStruct(rk.shape, bf),
            jax.ShapeDtypeStruct(rv.shape, bf),
        ),
        in_specs=[pl.BlockSpec(memory_space=pltpu.SMEM), vm, vm, vm, vm],
        out_specs=(vm, vm, vm, vm),
        scratch_shapes=[
            pltpu.VMEM((keys, columns), bf),
            pltpu.VMEM((keys, columns), bf),
            pltpu.VMEM((columns, keys), bf),
            pltpu.VMEM((columns, keys), bf),
            pltpu.VMEM((keys, QB), f32),
            pltpu.VMEM((keys, QB), bf),
            pltpu.VMEM((keys, columns), f32),
            pltpu.VMEM((keys, columns), f32),
        ],
        compiler_params=pltpu.CompilerParams(vmem_limit_bytes=40 * 2**20),
        name="attention",
    )(idx, q, rk, rv, da)


def scatter_kernel(chosen, filled, gk_ref, gv_ref, ok_ref, ov_ref, ak, av):
    ak[...] = jnp.zeros_like(ak)
    av[...] = jnp.zeros_like(av)
    for v in range(gk_ref.shape[0]):
        @pl.when(filled[v] != 0)
        def _():
            b = chosen[v]
            ak[b] = ak[b] + gk_ref[v].astype(jnp.float32)
            av[b] = av[b] + gv_ref[v].astype(jnp.float32)
    ok_ref[...] = ak[...].astype(jnp.bfloat16)
    ov_ref[...] = av[...].astype(jnp.bfloat16)


def scatter(chosen, filled, gk, gv, blocks):
    columns = gk.shape[2]
    vm = pl.BlockSpec(memory_space=pltpu.VMEM)
    sm = pl.BlockSpec(memory_space=pltpu.SMEM)
    out = jax.ShapeDtypeStruct((blocks, BLOCK, columns), jnp.bfloat16)
    return pl.pallas_call(
        scatter_kernel,
        out_shape=(out, out),
        in_specs=[sm, sm, vm, vm],
        out_specs=(vm, vm),
        scratch_shapes=[pltpu.VMEM((blocks, BLOCK, columns), jnp.float32)] * 2,
        name="scatter",
    )(chosen, filled, gk, gv)


def body(query_rows, key_rows, value_rows, out_weight, out_grad, source_view, source_block):
    tokens, columns = query_rows.shape
    blocks = tokens // BLOCK
    view = lax.axis_index("view")
    head = lax.axis_index("head")
    matched = source_view == view
    filled = jnp.any(matched, axis=1).astype(jnp.int32)
    chosen = jnp.sum(jnp.where(matched, source_block, 0), axis=1)
    own_view = lax.dynamic_index_in_dim(source_view, view, 0, keepdims=False)

    def fetch(rows):
        out = jnp.take(rows.reshape(blocks, BLOCK, columns), chosen, axis=0)
        return lax.all_to_all(out, "view", split_axis=0, concat_axis=0, tiled=True)

    rk = fetch(key_rows)
    rv = fetch(value_rows)
    og = lax.all_gather(out_grad, "head", axis=1, tiled=True)
    w_rows = lax.dynamic_slice_in_dim(out_weight, head * columns, columns, 0)
    da = lax.dot_general(
        og, w_rows, (((1,), (1,)), ((), ())), preferred_element_type=jnp.float32
    ).astype(jnp.bfloat16)
    att, dq, dk, dv = attention(own_view, query_rows, rk, rv, da)
    gk = lax.all_to_all(dk, "view", split_axis=0, concat_axis=0, tiled=True)
    gv = lax.all_to_all(dv, "view", split_axis=0, concat_axis=0, tiled=True)
    full = lax.all_gather(att, "head", axis=1, tiled=True)
    w_cols = lax.dynamic_slice_in_dim(out_weight, head * columns, columns, 1)
    mixed = dot(full, w_cols).astype(jnp.bfloat16)
    kg, vg = scatter(chosen, filled, gk, gv, blocks)
    return mixed, dq, kg.reshape(tokens, columns), vg.reshape(tokens, columns)


def solution(mesh):
    placed = (
        P("view", "head"),
        P("view", "head"),
        P("view", "head"),
        P(),
        P("view", "head"),
        P(),
        P(),
    )
    return jax.shard_map(
        body,
        mesh=mesh,
        in_specs=placed,
        out_specs=(P("view", "head"), P("view", "head"), P("view", "head"), P("view", "head")),
        check_vma=False,
    )
```

```python
import functools

import jax
import jax.numpy as jnp
from jax import lax
from jax.experimental import pallas as pl
from jax.experimental.pallas import tpu as pltpu
from jax.sharding import PartitionSpec as P

HEAD_DIM = 64
BLOCK = 128
SCALE = HEAD_DIM ** -0.5
LOG2E = 1.4426950408889634
QB = 256
KC = 256


def dot(a, b):
    return jnp.dot(a, b, preferred_element_type=jnp.float32)


MESH = pl.DeviceIdType.MESH
NZ, NY, NX = 8, 4, 4
NB = 8


class Copies:
    def __init__(self, send, recv):
        self.send, self.recv, self.n = send, recv, 0

    def make(self, src, dst, device):
        i = self.n
        self.n += 1
        return pltpu.make_async_remote_copy(
            src_ref=src,
            dst_ref=dst,
            send_sem=self.send.at[i],
            recv_sem=self.recv.at[i],
            device_id=device,
            device_id_type=MESH,
        )


class Place:
    def __init__(self):
        view = lax.axis_index("view")
        head = lax.axis_index("head")
        self.view, self.head = view, head
        self.z, self.y = view // NY, lax.rem(view, NY)
        self.x, self.c = head // 2, lax.rem(head, 2)

    def zplus(self, d):
        return lax.rem(self.z + d + NZ, NZ)

    def yplus(self, k):
        return lax.rem(self.y + k + NY, NY)

    def at_z(self, d):
        return {"view": self.zplus(d) * NY + self.y}

    def at_y(self, k):
        return {"view": self.z * NY + self.yplus(k)}

    def at_x(self, d):
        return {"head": lax.rem(self.x + d + NX, NX) * 2 + self.c}

    def partner(self):
        return {"head": self.x * 2 + 1 - self.c}

    def pick(self, table, dz, k, sz):
        taker = self.zplus(dz) * NY + self.yplus(k)
        return table[taker * (NZ * NY) + self.zplus(sz) * NY + self.y]

    def pick_abs(self, table, dz, yd, sz):
        taker = self.zplus(dz) * NY + yd
        return table[taker * (NZ * NY) + self.zplus(sz) * NY + self.y]


def greet(here, zy=True, x=True):
    barrier = pltpu.get_barrier_semaphore()
    peers = []
    if zy:
        peers += [here.at_z(1), here.at_z(-1), here.at_y(1), here.at_y(2), here.at_y(3)]
    if x:
        peers += [here.at_x(1), here.at_x(-1), here.partner()]
    for peer in peers:
        pl.semaphore_signal(barrier, inc=1, device_id=peer, device_id_type=MESH)
    pl.semaphore_wait(barrier, len(peers))


class Gather:
    def __init__(self, here, copies, own, full):
        rows = own.shape[0]
        half = rows // 2
        x, c = here.x, here.c
        me = here.head
        left = lax.rem(x + NX - 1, NX) * 2 + c
        right = lax.rem(x + 1, NX) * 2 + c
        far = lax.rem(x + 2, NX) * 2 + c
        lo, hi = pl.ds(0, half), pl.ds(half, half)
        self.own, self.full, self.me = own, full, me
        mk = copies.make
        self.first = [
            mk(own, full.at[me], here.at_x(1)),
            mk(own, full.at[me], here.at_x(-1)),
        ]
        self.second = [
            mk(full.at[left, lo], full.at[left, lo], here.at_x(1)),
            mk(full.at[right, hi], full.at[right, hi], here.at_x(-1)),
        ]
        self.across = [
            mk(own, full.at[me], here.partner()),
            mk(full.at[left], full.at[left], here.partner()),
            mk(full.at[right], full.at[right], here.partner()),
            mk(full.at[far], full.at[far], here.partner()),
        ]

    def step(self, n):
        if n == 0:
            for copy in self.first:
                copy.start()
            self.across[0].start()
            self.full[self.me] = self.own[...]
        if n == 1:
            for copy in self.first:
                copy.wait_recv()
            for copy in self.second:
                copy.start()
            self.across[1].start()
            self.across[2].start()
        if n == 2:
            for copy in self.second:
                copy.wait_recv()
            self.across[3].start()
        if n == 3:
            for copy in self.across:
                copy.wait_recv()
        if n == 4:
            for copy in self.first + self.second + self.across:
                copy.wait_send()


FETCH_PIECES = ((0, 1), (1, 3), (3, 5), (5, 8))


class Fetch:
    scratch = ((8, 2), (8, 2), (6, 2), (2, 2), (6, 2), (NB, 3))

    def __init__(self, here, copies, table, own, got, bufs):
        self.here, self.table, self.own, self.got = here, table, own, got
        one, two, three, four, fwd, stage = bufs
        self.one, self.two, self.three, self.four = one, two, three, four
        self.fwd, self.stage = fwd, stage
        mk = copies.make
        ways = (here.at_z(1), here.at_z(-1))
        h = NB // 2
        self.c1, self.c2, self.c3, self.c4 = [], [], [], []
        for part in range(2):
            for s, way in enumerate(ways):
                self.c1.append(mk(own.at[pl.ds(part * h, h)], one.at[s, pl.ds(part * h, h)], way))
        for part in range(2):
            for s, way in enumerate(ways):
                self.c2.append(
                    mk(one.at[s, pl.ds(part * h, h)], two.at[s, pl.ds(part * h, h)], way)
                )
        for s, way in enumerate(ways):
            self.c3.append(mk(fwd.at[s], three.at[s], way))
        for s, way in enumerate(ways):
            self.c4.append(mk(three.at[s, pl.ds(4, 2)], four.at[s], way))
        self.cy = []
        for a, b in FETCH_PIECES:
            self.cy.append(
                [
                    mk(stage.at[k - 1, pl.ds(a, b - a)], got.at[k, pl.ds(a, b - a)], here.at_y(k))
                    for k in (2, 1, 3)
                ]
            )

    def put(self, k, e, value):
        if k == 0:
            self.got[0, e] = value
        else:
            self.stage[k - 1, e] = value

    def select(self, src, k, sz):
        return src[jnp.maximum(self.here.pick(self.table, 0, k, sz), 0)]

    def start_y(self, piece):
        for copy in self.cy[piece]:
            copy.start()

    def step(self, n):
        here, table = self.here, self.table
        if n == 0:
            for copy in self.c1:
                copy.start()
            for k in range(NY):
                self.put(k, 0, self.select(self.own, k, 0))
            self.start_y(0)
        if n in (1, 2):
            part = n - 1
            for s in range(2):
                self.c1[part * 2 + s].wait_recv()
                self.c2[part * 2 + s].start()
        if n == 2:
            for k in range(NY):
                self.put(k, 1, self.select(self.one.at[0], k, -1))
                self.put(k, 2, self.select(self.one.at[1], k, 1))
            self.start_y(1)
        if n == 3:
            for copy in self.c2:
                copy.wait_recv()
            for s, d in ((0, 1), (1, -1)):
                src = self.two.at[s]
                for yd in range(4):
                    b = jnp.maximum(here.pick_abs(table, d, yd, -2 * d), 0)
                    self.fwd[s, yd] = src[b]
                for i in range(2):
                    b = jnp.maximum(here.pick_abs(table, 2 * d, 2 * s + i, -2 * d), 0)
                    self.fwd[s, 4 + i] = src[b]
            for k in range(NY):
                self.put(k, 3, self.select(self.two.at[0], k, -2))
                self.put(k, 4, self.select(self.two.at[1], k, 2))
            for copy in self.c3:
                copy.start()
            self.start_y(2)
        if n == 4:
            for s in range(2):
                self.c3[s].wait_recv()
                self.c4[s].start()
            for k in range(NY):
                yd = here.yplus(k)
                self.put(k, 5, self.three[0, yd])
                self.put(k, 6, self.three[1, yd])
        if n == 5:
            for copy in self.c4:
                copy.wait_recv()
            for k in range(NY):
                yd = here.yplus(k)
                low = lax.rem(yd, 2)
                self.put(k, 7, jnp.where(yd < 2, self.four[0, low], self.four[1, low]))
            self.start_y(3)
        if n == 6:
            for piece in self.cy:
                for copy in piece:
                    copy.wait_recv()
        if n == 7:
            for copy in self.c1 + self.c2 + self.c3 + self.c4:
                copy.wait_send()
            for piece in self.cy:
                for copy in piece:
                    copy.wait_send()


RETURN_PIECES = ((5, 8), (3, 5), (1, 3), (0, 1))


class Return:
    scratch = ((2, 2), (6, 2), (8, 2), (8, 2), (8, 2), (8, 2))

    def __init__(self, here, copies, table, sent, held, out, bufs):
        self.here, self.table, self.held, self.out = here, table, held, out
        four, three, two, one, out2, out1 = bufs
        self.four, self.three, self.two, self.one = four, three, two, one
        self.out2, self.out1 = out2, out1
        mk = copies.make
        ways = (here.at_z(-1), here.at_z(1))
        h = NB // 2
        self.cy = []
        for a, b in RETURN_PIECES:
            self.cy.append(
                [
                    mk(sent.at[k - 1, pl.ds(a, b - a)], held.at[k, pl.ds(a, b - a)], here.at_y(-k))
                    for k in (2, 1, 3)
                ]
            )
        self.c4, self.c3, self.c2, self.c1 = [], [], [], []
        for s, way in enumerate(ways):
            for i in range(2):
                k = lax.rem(2 * s + i + NY - here.y, NY)
                self.c4.append(mk(held.at[k, 7], four.at[s, i], way))
        for s, way in enumerate(ways):
            self.c3.append(mk(held.at[:, 5 + s], three.at[s, pl.ds(0, 4)], way))
        for s, way in enumerate(ways):
            self.c3.append(mk(four.at[s], three.at[s, pl.ds(4, 2)], way))
        for part in range(2):
            for s, way in enumerate(ways):
                self.c2.append(
                    mk(out2.at[s, pl.ds(part * h, h)], two.at[s, pl.ds(part * h, h)], way)
                )
        for part in range(2):
            for s, way in enumerate(ways):
                self.c1.append(
                    mk(out1.at[s, pl.ds(part * h, h)], one.at[s, pl.ds(part * h, h)], way)
                )

    def start_y(self, piece):
        for copy in self.cy[piece]:
            copy.start()

    def wait_y(self, piece):
        for copy in self.cy[piece]:
            copy.wait_recv()

    @staticmethod
    def total(b, bases, terms):
        acc = None
        for value in bases:
            value = value.astype(jnp.float32)
            acc = value if acc is None else acc + value
        for pick, ref in terms:
            value = ref[...].astype(jnp.float32)
            value = jnp.where(pick == b, value, jnp.zeros_like(value))
            acc = value if acc is None else acc + value
        return acc.astype(jnp.bfloat16)

    def here_terms(self, e, sz):
        return [
            (self.here.pick(self.table, 0, k, sz), self.held.at[k, e]) for k in range(NY)
        ]

    def step(self, n):
        here, table = self.here, self.table
        h = NB // 2
        if n == 0:
            for piece in range(4):
                self.start_y(piece)
        if n == 1:
            self.wait_y(0)
            for copy in self.c4 + self.c3[:2]:
                copy.start()
        if n == 2:
            for copy in self.c4:
                copy.wait_recv()
            for copy in self.c3[2:]:
                copy.start()
        if n == 3:
            self.wait_y(1)
            for copy in self.c3:
                copy.wait_recv()
            for part in range(2):
                for s, d in ((0, 1), (1, -1)):
                    terms = self.here_terms(3 + s, -2 * d)
                    for k in range(4):
                        terms.append((here.pick(table, d, k, -2 * d), self.three.at[s, k]))
                    for i in range(2):
                        pick = here.pick_abs(table, 2 * d, 2 * s + i, -2 * d)
                        terms.append((pick, self.three.at[s, 4 + i]))
                    for b in range(part * h, part * h + h):
                        self.out2[s, b] = self.total(b, [], terms)
                for s in range(2):
                    self.c2[part * 2 + s].start()
        if n in (4, 5):
            part = n - 4
            if n == 4:
                self.wait_y(2)
            for s, d in ((0, 1), (1, -1)):
                self.c2[part * 2 + s].wait_recv()
                terms = self.here_terms(1 + s, -d)
                for b in range(part * h, part * h + h):
                    self.out1[s, b] = self.total(b, [self.two[s, b]], terms)
            for s in range(2):
                self.c1[part * 2 + s].start()
        if n in (6, 7):
            part = n - 6
            if n == 6:
                self.wait_y(3)
            for s in range(2):
                self.c1[part * 2 + s].wait_recv()
            terms = self.here_terms(0, 0)
            for b in range(part * h, part * h + h):
                self.out[b] = self.total(b, [self.one[0, b], self.one[1, b]], terms)
        if n == 8:
            for copy in self.c4 + self.c3 + self.c2 + self.c1:
                copy.wait_send()
            for piece in self.cy:
                for copy in piece:
                    copy.wait_send()


def attention_kernel(
    idx, q_ref, rk_ref, rv_ref, og_ref, w_ref,
    att_ref, dq_ref, dk_ref, dv_ref,
    k_s, v_s, kt_s, vt_s, s_s, p_s, dk_a, dv_a,
):
    slots = idx.shape[0]
    keys = slots * BLOCK
    tokens = q_ref.shape[0]
    for j in range(slots):
        rows = pl.ds(j * BLOCK, BLOCK)
        kb = rk_ref[idx[j]]
        vb = rv_ref[idx[j]]
        k_s[rows, :] = kb
        v_s[rows, :] = vb
        kt_s[:, rows] = kb.T
        vt_s[:, rows] = vb.T
    dk_a[...] = jnp.zeros_like(dk_a)
    dv_a[...] = jnp.zeros_like(dv_a)
    chunks = keys // KC
    lane = lax.broadcasted_iota(jnp.int32, (QB, 2 * HEAD_DIM), 1)

    def step(i, carry):
        qrows = pl.ds(pl.multiple_of(i * QB, QB), QB)
        q = q_ref[qrows, :]
        da = None
        for g in range(og_ref.shape[0]):
            cols = pl.ds(g * 2 * HEAD_DIM, 2 * HEAD_DIM)
            part = lax.dot_general(
                og_ref[g, qrows, :], w_ref[:, cols], (((1,), (1,)), ((), ())),
                preferred_element_type=jnp.float32,
            )
            da = part if da is None else da + part
        da = da.astype(jnp.bfloat16)
        qt = q.T
        dat = da.T
        atts = []
        dqs = []
        for h in range(2):
            hd = slice(h * HEAD_DIM, (h + 1) * HEAD_DIM)
            mine = (lane // HEAD_DIM) == h
            qh = jnp.where(mine, q, jnp.zeros_like(q))
            dah = jnp.where(mine, da, jnp.zeros_like(da))
            qth = qt[hd, :]
            dath = dat[hd, :]
            top = None
            for c in range(chunks):
                rows = pl.ds(c * KC, KC)
                s = dot(k_s[rows, hd], qth)
                s_s[rows, :] = s
                m = jnp.max(s, axis=0, keepdims=True)
                top = m if top is None else jnp.maximum(top, m)
            shift = top * (SCALE * LOG2E)
            total = jnp.zeros((1, QB), jnp.float32)
            for c in range(chunks):
                rows = pl.ds(c * KC, KC)
                e = jnp.exp2(s_s[rows, :] * (SCALE * LOG2E) - shift)
                s_s[rows, :] = e
                total = total + jnp.sum(e, axis=0, keepdims=True)
            inv = 1.0 / total
            for c in range(chunks):
                rows = pl.ds(c * KC, KC)
                p = s_s[rows, :] * inv
                pb = p.astype(jnp.bfloat16)
                p_s[rows, :] = pb
                dv_a[rows, :] += dot(pb, dah)
            att = dot(vt_s[hd, :], p_s[...]).astype(jnp.bfloat16)
            atts.append(att)
            delta = jnp.sum(
                att.astype(jnp.float32) * dath.astype(jnp.float32), axis=0, keepdims=True
            )
            for c in range(chunks):
                rows = pl.ds(c * KC, KC)
                dp = dot(v_s[rows, hd], dath)
                ds = ((s_s[rows, :] * inv) * (dp - delta)).astype(jnp.bfloat16)
                p_s[rows, :] = ds
                dk_a[rows, :] += dot(ds, qh)
            dqs.append(dot(kt_s[hd, :], p_s[...]) * SCALE)
        att_ref[qrows, :] = jnp.concatenate(atts, axis=0).T
        dq_ref[qrows, :] = jnp.concatenate(dqs, axis=0).astype(jnp.bfloat16).T
        return carry

    lax.fori_loop(0, tokens // QB, step, 0)
    for j in range(slots):
        rows = pl.ds(j * BLOCK, BLOCK)
        dk_ref[idx[j]] = (dk_a[rows, :] * SCALE).astype(jnp.bfloat16)
        dv_ref[idx[j]] = dv_a[rows, :].astype(jnp.bfloat16)


def attention(idx, q, rk, rv, og, w_rows):
    tokens, columns = q.shape
    keys = idx.shape[0] * BLOCK
    vm = pl.BlockSpec(memory_space=pltpu.VMEM)
    bf, f32 = jnp.bfloat16, jnp.float32
    return pl.pallas_call(
        attention_kernel,
        out_shape=(
            jax.ShapeDtypeStruct((tokens, columns), bf),
            jax.ShapeDtypeStruct((tokens, columns), bf),
            jax.ShapeDtypeStruct(rk.shape, bf),
            jax.ShapeDtypeStruct(rv.shape, bf),
        ),
        in_specs=[pl.BlockSpec(memory_space=pltpu.SMEM), vm, vm, vm, vm, vm],
        out_specs=(vm, vm, vm, vm),
        scratch_shapes=[
            pltpu.VMEM((keys, columns), bf),
            pltpu.VMEM((keys, columns), bf),
            pltpu.VMEM((columns, keys), bf),
            pltpu.VMEM((columns, keys), bf),
            pltpu.VMEM((keys, QB), f32),
            pltpu.VMEM((keys, QB), bf),
            pltpu.VMEM((keys, columns), f32),
            pltpu.VMEM((keys, columns), f32),
        ],
        compiler_params=pltpu.CompilerParams(vmem_limit_bytes=40 * 2**20),
        name="attention",
    )(idx, q, rk, rv, og, w_rows)


def fetch_kernel(table, og_ref, k_ref, v_ref, gk_ref, gv_ref, full_ref, *scratch):
    bk, bv, (send, recv) = scratch[:6], scratch[6:12], scratch[12:]
    here = Place()
    copies = Copies(send, recv)
    og = Gather(here, copies, og_ref, full_ref)
    fk = Fetch(here, copies, table, k_ref, gk_ref, bk)
    fv = Fetch(here, copies, table, v_ref, gv_ref, bv)
    greet(here)
    fk.step(0)
    og.step(0)
    fv.step(0)
    fk.step(1)
    fk.step(2)
    fv.step(1)
    fv.step(2)
    og.step(1)
    fk.step(3)
    fk.step(4)
    fv.step(3)
    og.step(2)
    fk.step(5)
    fv.step(4)
    fv.step(5)
    og.step(3)
    fk.step(6)
    fv.step(6)
    fk.step(7)
    fv.step(7)
    og.step(4)


def fetch_scratch():
    return [pltpu.VMEM((b, a, BLOCK, 2 * HEAD_DIM), jnp.bfloat16) for a, b in Fetch.scratch]


def fetch(table, og, k, v):
    bf = jnp.bfloat16
    tokens, columns = og.shape
    vm = pl.BlockSpec(memory_space=pltpu.VMEM)
    got = jax.ShapeDtypeStruct((NY, NZ, BLOCK, columns), bf)
    return pl.pallas_call(
        fetch_kernel,
        out_shape=(got, got, jax.ShapeDtypeStruct((2 * NX, tokens, columns), bf)),
        in_specs=[pl.BlockSpec(memory_space=pltpu.SMEM), vm, vm, vm],
        out_specs=(vm, vm, vm),
        scratch_shapes=fetch_scratch() + fetch_scratch()
        + [pltpu.SemaphoreType.DMA((64,)), pltpu.SemaphoreType.DMA((64,))],
        compiler_params=pltpu.CompilerParams(
            collective_id=0, has_side_effects=True, vmem_limit_bytes=40 * 2**20
        ),
        name="fetch",
    )(table, og, k, v)


def return_kernel(table, att_ref, w_ref, ck_ref, cv_ref, mixed_ref, ok_ref, ov_ref, *scratch):
    bk, bv = scratch[:6], scratch[6:12]
    full, hk, hv, send, recv = scratch[12:]
    here = Place()
    copies = Copies(send, recv)
    hk[0] = ck_ref[0]
    hv[0] = cv_ref[0]
    at = Gather(here, copies, att_ref, full)
    rk = Return(here, copies, table, ck_ref.at[pl.ds(1, 3)], hk, ok_ref, bk)
    rv = Return(here, copies, table, cv_ref.at[pl.ds(1, 3)], hv, ov_ref, bv)
    greet(here)
    rk.step(0)
    rv.step(0)
    at.step(0)
    rk.step(1)
    rk.step(2)
    rv.step(1)
    rv.step(2)
    at.step(1)
    rk.step(3)
    at.step(2)
    rv.step(3)
    at.step(3)

    def mix(i, carry):
        rows = pl.ds(pl.multiple_of(i * QB, QB), QB)
        acc = None
        for g in range(2 * NX):
            part = dot(full[g, rows, :], w_ref[pl.ds(g * 2 * HEAD_DIM, 2 * HEAD_DIM), :])
            acc = part if acc is None else acc + part
        mixed_ref[rows, :] = acc.astype(jnp.bfloat16)
        return carry

    lax.fori_loop(0, mixed_ref.shape[0] // QB, mix, 0)
    rk.step(4)
    rk.step(5)
    rv.step(4)
    rv.step(5)
    rk.step(6)
    rk.step(7)
    rv.step(6)
    rv.step(7)
    rk.step(8)
    rv.step(8)
    at.step(4)


def give_back(table, att, w_cols, ck, cv):
    bf = jnp.bfloat16
    tokens, columns = att.shape
    vm = pl.BlockSpec(memory_space=pltpu.VMEM)
    out = jax.ShapeDtypeStruct((NB, BLOCK, columns), bf)
    bufs = [pltpu.VMEM((b, a, BLOCK, columns), bf) for a, b in Return.scratch]
    return pl.pallas_call(
        return_kernel,
        out_shape=(jax.ShapeDtypeStruct((tokens, columns), bf), out, out),
        in_specs=[pl.BlockSpec(memory_space=pltpu.SMEM), vm, vm, vm, vm],
        out_specs=(vm, vm, vm),
        scratch_shapes=bufs + bufs + [
            pltpu.VMEM((2 * NX, tokens, columns), bf),
            pltpu.VMEM((NY, NZ, BLOCK, columns), bf),
            pltpu.VMEM((NY, NZ, BLOCK, columns), bf),
            pltpu.SemaphoreType.DMA((64,)),
            pltpu.SemaphoreType.DMA((64,)),
        ],
        compiler_params=pltpu.CompilerParams(
            collective_id=1, has_side_effects=True, vmem_limit_bytes=40 * 2**20
        ),
        name="give_back",
    )(table, att, w_cols, ck, cv)


def routes(source_view, source_block):
    view = lax.axis_index("view")
    views = jnp.arange(NZ * NY, dtype=jnp.int32)
    same = source_view[:, :, None] == views[None, None, :]
    table = jnp.max(jnp.where(same, source_block[:, :, None], -1), axis=1).reshape(-1)
    mine = lax.dynamic_index_in_dim(source_view, view, 0, keepdims=False)
    dz = lax.rem(view // NY - mine // NY + NZ, NZ)
    dy = lax.rem(lax.rem(view, NY) - lax.rem(mine, NY) + NY, NY)
    place = dy * NZ + jnp.where(dz == 0, 0, jnp.where(dz <= 4, 2 * dz - 1, 16 - 2 * dz))
    return table, place


def body(query_rows, key_rows, value_rows, out_weight, out_grad, source_view, source_block):
    tokens, columns = query_rows.shape
    head = lax.axis_index("head")
    table, place = routes(source_view, source_block)
    cut = (NB, BLOCK, columns)
    got_k, got_v, og = fetch(table, out_grad, key_rows.reshape(cut), value_rows.reshape(cut))
    flat = (NY * NZ, BLOCK, columns)
    w_rows = lax.dynamic_slice_in_dim(out_weight, head * columns, columns, 0)
    w_cols = lax.dynamic_slice_in_dim(out_weight, head * columns, columns, 1)
    att, dq, ck, cv = attention(
        place, query_rows, got_k.reshape(flat), got_v.reshape(flat), og, w_rows
    )
    mixed, kg, vg = give_back(table, att, w_cols, ck.reshape(got_k.shape), cv.reshape(got_v.shape))
    return mixed, dq, kg.reshape(tokens, columns), vg.reshape(tokens, columns)


def solution(mesh):
    spread = P("view", "head")
    return jax.shard_map(
        body,
        mesh=mesh,
        in_specs=(spread, spread, spread, P(), spread, P(), P()),
        out_specs=(spread, spread, spread, spread),
        check_vma=False,
    )
```

```python
import jax
import jax.numpy as jnp
from jax import lax
from jax.experimental import pallas as pl
from jax.experimental.pallas import tpu as pltpu
from jax.sharding import PartitionSpec as P

HEAD_DIM = 64
BLOCK = 128
COLS = 2 * HEAD_DIM
SCALE = HEAD_DIM ** -0.5
LOG2E = 1.4426950408889634
QB = 256
KC = 256
BF = jnp.bfloat16
F32 = jnp.float32


def dot(a, b):
    return jnp.dot(a, b, preferred_element_type=jnp.float32)


MESH = pl.DeviceIdType.MESH
NZ, NY, NX = 8, 4, 4
NB = 8


class Copies:
    def __init__(self, send, recv):
        self.send, self.recv, self.n = send, recv, 0

    def make(self, src, dst, device):
        i = self.n
        self.n += 1
        return pltpu.make_async_remote_copy(
            src_ref=src,
            dst_ref=dst,
            send_sem=self.send.at[i],
            recv_sem=self.recv.at[i],
            device_id=device,
            device_id_type=MESH,
        )


class Place:
    def __init__(self):
        view = lax.axis_index("view")
        head = lax.axis_index("head")
        self.view, self.head = view, head
        self.z, self.y = view // NY, lax.rem(view, NY)
        self.x, self.c = head // 2, lax.rem(head, 2)

    def zplus(self, d):
        return lax.rem(self.z + d + NZ, NZ)

    def yplus(self, k):
        return lax.rem(self.y + k + NY, NY)

    def at_z(self, d):
        return {"view": self.zplus(d) * NY + self.y}

    def at_y(self, k):
        return {"view": self.z * NY + self.yplus(k)}

    def at_x(self, d):
        return {"head": lax.rem(self.x + d + NX, NX) * 2 + self.c}

    def partner(self):
        return {"head": self.x * 2 + 1 - self.c}

    def pick(self, table, dz, k, sz):
        taker = self.zplus(dz) * NY + self.yplus(k)
        return table[taker * (NZ * NY) + self.zplus(sz) * NY + self.y]

    def pick_abs(self, table, dz, yd, sz):
        taker = self.zplus(dz) * NY + yd
        return table[taker * (NZ * NY) + self.zplus(sz) * NY + self.y]


def greet(here, zy=True, x=True):
    barrier = pltpu.get_barrier_semaphore()
    peers = []
    if zy:
        peers += [here.at_z(1), here.at_z(-1), here.at_y(1), here.at_y(2), here.at_y(3)]
    if x:
        peers += [here.at_x(1), here.at_x(-1), here.partner()]
    for peer in peers:
        pl.semaphore_signal(barrier, inc=1, device_id=peer, device_id_type=MESH)
    pl.semaphore_wait(barrier, len(peers))


class Gather:
    def __init__(self, here, copies, own, full):
        rows = own.shape[0]
        half = rows // 2
        x, c = here.x, here.c
        me = here.head
        left = lax.rem(x + NX - 1, NX) * 2 + c
        right = lax.rem(x + 1, NX) * 2 + c
        far = lax.rem(x + 2, NX) * 2 + c
        lo, hi = pl.ds(0, half), pl.ds(half, half)
        self.own, self.full, self.me = own, full, me
        mk = copies.make
        self.first = [
            mk(own, full.at[me], here.at_x(1)),
            mk(own, full.at[me], here.at_x(-1)),
        ]
        self.second = [
            mk(full.at[left, lo], full.at[left, lo], here.at_x(1)),
            mk(full.at[right, hi], full.at[right, hi], here.at_x(-1)),
        ]
        self.across = [
            mk(own, full.at[me], here.partner()),
            mk(full.at[left], full.at[left], here.partner()),
            mk(full.at[right], full.at[right], here.partner()),
            mk(full.at[far], full.at[far], here.partner()),
        ]

    def step(self, n):
        if n == 0:
            for copy in self.first:
                copy.start()
            self.across[0].start()
            self.full[self.me] = self.own[...]
        if n == 1:
            for copy in self.first:
                copy.wait_recv()
            for copy in self.second:
                copy.start()
            self.across[1].start()
            self.across[2].start()
        if n == 2:
            for copy in self.second:
                copy.wait_recv()
            self.across[3].start()
        if n == 3:
            for copy in self.across:
                copy.wait_recv()
        if n == 4:
            for copy in self.first + self.second + self.across:
                copy.wait_send()


FETCH_PIECES = ((0, 1), (1, 3), (3, 5), (5, 7), (7, 8))


class Fetch:
    scratch = ((8, 2), (8, 2), (6, 2), (2, 2), (6, 2), (NB, 3))

    def __init__(self, here, copies, table, own, got, bufs):
        self.here, self.table, self.own, self.got = here, table, own, got
        one, two, three, four, fwd, stage = bufs
        self.one, self.two, self.three, self.four = one, two, three, four
        self.fwd, self.stage = fwd, stage
        mk = copies.make
        ways = (here.at_z(1), here.at_z(-1))
        h = NB // 2
        self.c1, self.c2, self.c3, self.c4 = [], [], [], []
        for part in range(2):
            for s, way in enumerate(ways):
                self.c1.append(mk(own.at[pl.ds(part * h, h)], one.at[s, pl.ds(part * h, h)], way))
        for part in range(2):
            for s, way in enumerate(ways):
                self.c2.append(
                    mk(one.at[s, pl.ds(part * h, h)], two.at[s, pl.ds(part * h, h)], way)
                )
        for s, way in enumerate(ways):
            self.c3.append(mk(fwd.at[s], three.at[s], way))
        for s, way in enumerate(ways):
            self.c4.append(mk(three.at[s, pl.ds(4, 2)], four.at[s], way))
        self.cy = []
        for a, b in FETCH_PIECES:
            self.cy.append(
                [
                    mk(
                        stage.at[k - 1, pl.ds(a, b - a)],
                        got.at[pl.ds(k * NZ + a, b - a)],
                        here.at_y(k),
                    )
                    for k in (2, 1, 3)
                ]
            )

    def put(self, k, e, value):
        if k == 0:
            self.got[e] = value
        else:
            self.stage[k - 1, e] = value

    def select(self, src, k, sz):
        return src[jnp.maximum(self.here.pick(self.table, 0, k, sz), 0)]

    def start_y(self, piece):
        for copy in self.cy[piece]:
            copy.start()

    def offer(self, part):
        for copy in self.c1[part * 2 : part * 2 + 2]:
            copy.start()

    def step(self, n):
        here, table = self.here, self.table
        if n == 0:
            for k in range(NY):
                self.put(k, 0, self.select(self.own, k, 0))
            self.start_y(0)
        if n in (1, 2):
            part = n - 1
            for s in range(2):
                self.c1[part * 2 + s].wait_recv()
                self.c2[part * 2 + s].start()
        if n == 2:
            for k in range(NY):
                self.put(k, 1, self.select(self.one.at[0], k, -1))
                self.put(k, 2, self.select(self.one.at[1], k, 1))
            self.start_y(1)
        if n == 3:
            for copy in self.c2:
                copy.wait_recv()
            for s, d in ((0, 1), (1, -1)):
                src = self.two.at[s]
                for yd in range(4):
                    b = jnp.maximum(here.pick_abs(table, d, yd, -2 * d), 0)
                    self.fwd[s, yd] = src[b]
                for i in range(2):
                    b = jnp.maximum(here.pick_abs(table, 2 * d, 2 * s + i, -2 * d), 0)
                    self.fwd[s, 4 + i] = src[b]
            for k in range(NY):
                self.put(k, 3, self.select(self.two.at[0], k, -2))
                self.put(k, 4, self.select(self.two.at[1], k, 2))
            for copy in self.c3:
                copy.start()
            self.start_y(2)
        if n == 4:
            for s in range(2):
                self.c3[s].wait_recv()
                self.c4[s].start()
            for k in range(NY):
                yd = here.yplus(k)
                self.put(k, 5, self.three[0, yd])
                self.put(k, 6, self.three[1, yd])
            self.start_y(3)
        if n == 5:
            for copy in self.c4:
                copy.wait_recv()
            for k in range(NY):
                yd = here.yplus(k)
                low = lax.rem(yd, 2)
                self.put(k, 7, jnp.where(yd < 2, self.four[0, low], self.four[1, low]))
            self.start_y(4)
        if n == 6:
            for piece in self.cy:
                for copy in piece:
                    copy.wait_recv()
        if n == 7:
            for copy in self.c1 + self.c2 + self.c3 + self.c4:
                copy.wait_send()
            for piece in self.cy:
                for copy in piece:
                    copy.wait_send()


RETURN_PIECES = ((5, 8), (3, 5), (1, 3), (0, 1))


class Return:
    scratch = ((2, 2), (6, 2), (8, 2), (8, 2), (8, 2), (8, 2))

    def __init__(self, here, copies, table, sent, held, out, bufs):
        self.here, self.table, self.held, self.out = here, table, held, out
        four, three, two, one, out2, out1 = bufs
        self.four, self.three, self.two, self.one = four, three, two, one
        self.out2, self.out1 = out2, out1
        mk = copies.make
        ways = (here.at_z(-1), here.at_z(1))
        h = NB // 2
        self.cy = []
        for a, b in RETURN_PIECES:
            self.cy.append(
                [
                    mk(sent.at[k - 1, pl.ds(a, b - a)], held.at[k, pl.ds(a, b - a)], here.at_y(-k))
                    for k in (2, 1, 3)
                ]
            )
        self.c4, self.c3, self.c2, self.c1 = [], [], [], []
        for s, way in enumerate(ways):
            for i in range(2):
                k = lax.rem(2 * s + i + NY - here.y, NY)
                self.c4.append(mk(held.at[k, 7], four.at[s, i], way))
        for s, way in enumerate(ways):
            self.c3.append(mk(held.at[:, 5 + s], three.at[s, pl.ds(0, 4)], way))
        for s, way in enumerate(ways):
            self.c3.append(mk(four.at[s], three.at[s, pl.ds(4, 2)], way))
        for part in range(2):
            for s, way in enumerate(ways):
                self.c2.append(
                    mk(out2.at[s, pl.ds(part * h, h)], two.at[s, pl.ds(part * h, h)], way)
                )
        for part in range(2):
            for s, way in enumerate(ways):
                self.c1.append(
                    mk(out1.at[s, pl.ds(part * h, h)], one.at[s, pl.ds(part * h, h)], way)
                )

    def start_y(self, piece):
        for copy in self.cy[piece]:
            copy.start()

    def wait_y(self, piece):
        for copy in self.cy[piece]:
            copy.wait_recv()

    @staticmethod
    def total(b, bases, terms):
        acc = None
        for value in bases:
            value = value.astype(jnp.float32)
            acc = value if acc is None else acc + value
        for pick, ref in terms:
            value = ref[...].astype(jnp.float32)
            value = jnp.where(pick == b, value, jnp.zeros_like(value))
            acc = value if acc is None else acc + value
        return acc.astype(jnp.bfloat16)

    def here_terms(self, e, sz):
        return [
            (self.here.pick(self.table, 0, k, sz), self.held.at[k, e]) for k in range(NY)
        ]

    def step(self, n):
        here, table = self.here, self.table
        h = NB // 2
        if n == 0:
            for piece in range(4):
                self.start_y(piece)
        if n == 1:
            self.wait_y(0)
            for copy in self.c4 + self.c3[:2]:
                copy.start()
        if n == 2:
            for copy in self.c4:
                copy.wait_recv()
            for copy in self.c3[2:]:
                copy.start()
        if n == 3:
            self.wait_y(1)
            for copy in self.c3:
                copy.wait_recv()
            for part in range(2):
                for s, d in ((0, 1), (1, -1)):
                    terms = self.here_terms(3 + s, -2 * d)
                    for k in range(4):
                        terms.append((here.pick(table, d, k, -2 * d), self.three.at[s, k]))
                    for i in range(2):
                        pick = here.pick_abs(table, 2 * d, 2 * s + i, -2 * d)
                        terms.append((pick, self.three.at[s, 4 + i]))
                    for b in range(part * h, part * h + h):
                        self.out2[s, b] = self.total(b, [], terms)
                for s in range(2):
                    self.c2[part * 2 + s].start()
        if n in (4, 5):
            part = n - 4
            if n == 4:
                self.wait_y(2)
            for s, d in ((0, 1), (1, -1)):
                self.c2[part * 2 + s].wait_recv()
                terms = self.here_terms(1 + s, -d)
                for b in range(part * h, part * h + h):
                    self.out1[s, b] = self.total(b, [self.two[s, b]], terms)
            for s in range(2):
                self.c1[part * 2 + s].start()
        if n in (6, 7):
            part = n - 6
            if n == 6:
                self.wait_y(3)
            for s in range(2):
                self.c1[part * 2 + s].wait_recv()
            terms = self.here_terms(0, 0)
            for b in range(part * h, part * h + h):
                self.out[b] = self.total(b, [self.one[0, b], self.one[1, b]], terms)
        if n == 8:
            for copy in self.c4 + self.c3 + self.c2 + self.c1:
                copy.wait_send()
            for piece in self.cy:
                for copy in piece:
                    copy.wait_send()


def rows_at(i, size):
    return pl.ds(pl.multiple_of(i * size, size), size)


def layer_kernel(
    table, place, slot_of,
    q_hbm, k_hbm, v_hbm, w_hbm, og_hbm,
    mixed_hbm, dq_hbm, ok_hbm, ov_hbm,
    *scratch,
):
    fbk, fbv, rbk, rbv = scratch[:6], scratch[6:12], scratch[12:18], scratch[18:24]
    (
        k_own, v_own, og_own, q_s, w_rows, w_cols,
        got_k, got_v, og_all, at_all, sent_k, sent_v, held_k, held_v,
        qm, qtm, dam, datm, k_s, kt_s, v_s, vt_s, s_s, p_s,
        att_t, dq_t, grad_s, att_s, dq_s, mixed_s, ok_s, ov_s,
        send, recv, local,
    ) = scratch[24:]
    here = Place()
    copies = Copies(send, recv)
    slots = place.shape[0]
    keys = slots * BLOCK
    tokens = q_s.shape[0]
    chunks = keys // KC
    mine = pl.ds(pl.multiple_of(here.head * COLS, COLS), COLS)

    loads = [
        pltpu.make_async_copy(src, dst, local.at[i])
        for i, (src, dst) in enumerate(
            (
                (k_hbm, k_own),
                (og_hbm, og_own),
                (v_hbm, v_own),
                (q_hbm, q_s),
                (w_hbm.at[mine, :], w_rows),
                (w_hbm.at[:, mine], w_cols),
            )
        )
    ]
    stores = [
        pltpu.make_async_copy(src, dst, local.at[len(loads) + i])
        for i, (src, dst) in enumerate(
            ((dq_s, dq_hbm), (mixed_s, mixed_hbm), (ov_s, ov_hbm), (ok_s, ok_hbm))
        )
    ]
    for load in loads:
        load.start()

    og = Gather(here, copies, og_own, og_all)
    fk = Fetch(here, copies, table, k_own, got_k, fbk)
    fv = Fetch(here, copies, table, v_own, got_v, fbv)
    at = Gather(here, copies, att_s, at_all)
    rk = Return(here, copies, table, sent_k, held_k, ok_s, rbk)
    rv = Return(here, copies, table, sent_v, held_v, ov_s, rbv)

    greet(here)
    loads[0].wait()
    fk.offer(0)
    fk.offer(1)
    loads[1].wait()
    og.step(0)
    fk.step(0)
    loads[2].wait()
    fv.step(0)
    loads[3].wait()
    q = q_s[...]
    lane = lax.broadcasted_iota(jnp.int32, q.shape, 1) // HEAD_DIM
    for h in range(2):
        part = jnp.where(lane == h, q, jnp.zeros_like(q))
        qm[h] = part
        qtm[h] = part.T
    fk.step(1)
    fk.step(2)
    fv.offer(0)
    og.step(1)
    fk.step(3)
    fv.offer(1)
    og.step(2)
    loads[4].wait()
    og.step(3)

    def project(i, carry):
        rows = rows_at(i, QB)
        acc = None
        for g in range(2 * NX):
            part = lax.dot_general(
                og_all[g, rows, :],
                w_rows[:, pl.ds(g * COLS, COLS)],
                (((1,), (1,)), ((), ())),
                preferred_element_type=jnp.float32,
            )
            acc = part if acc is None else acc + part
        da = acc.astype(BF)
        half = lax.broadcasted_iota(jnp.int32, da.shape, 1) // HEAD_DIM
        for h in range(2):
            part = jnp.where(half == h, da, jnp.zeros_like(da))
            dam[h, rows, :] = part
            datm[h, :, rows] = part.T
        return carry

    lax.fori_loop(0, tokens // QB, project, 0)
    fk.step(4)
    fv.step(1)
    fk.step(5)
    fv.step(2)
    fk.step(6)
    for j in range(slots):
        rows = pl.ds(j * BLOCK, BLOCK)
        block = got_k[place[j]]
        k_s[rows, :] = block
        kt_s[:, rows] = block.T

    steps = 2 * (tokens // QB)

    def forward(i, carry):
        for n, at_step in ((3, 2), (4, 6), (5, 7)):
            @pl.when(i == at_step)
            def _():
                fv.step(n)

        h = lax.rem(i, 2)
        cols = rows_at(i // 2, QB)
        qt = qtm[h, :, cols]
        top = None
        for c in range(chunks):
            rows = pl.ds(c * KC, KC)
            s = dot(k_s[rows, :], qt)
            s_s[rows, :] = s
            m = jnp.max(s, axis=0, keepdims=True)
            top = m if top is None else jnp.maximum(top, m)
        shift = top * (SCALE * LOG2E)
        total = jnp.zeros((1, QB), F32)
        for c in range(chunks):
            rows = pl.ds(c * KC, KC)
            e = jnp.exp2(s_s[rows, :] * (SCALE * LOG2E) - shift)
            s_s[rows, :] = e
            total = total + jnp.sum(e, axis=0, keepdims=True)
        inv = 1.0 / total
        for c in range(chunks):
            rows = pl.ds(c * KC, KC)
            p_s[h, rows, cols] = (s_s[rows, :] * inv).astype(BF)
        return carry

    lax.fori_loop(0, steps, forward, 0)

    def contract(scale, right):
        def one(c, carry):
            rows = rows_at(c, KC)
            g = dot(p_s[0, rows, :], right[0]) + dot(p_s[1, rows, :], right[1])
            if scale is not None:
                g = g * scale
            g = g.astype(BF)
            for b in range(KC // BLOCK):
                grad_s[c * (KC // BLOCK) + b] = g[b * BLOCK : (b + 1) * BLOCK, :]
            return carry

        lax.fori_loop(0, chunks, one, 0)

    def hand_out(sent, held):
        for e in range(NZ):
            held[0, e] = grad_s[slot_of[e]]
        for k in range(1, NY):
            for e in range(NZ):
                sent[k - 1, e] = grad_s[slot_of[k * NZ + e]]

    contract(None, dam)
    hand_out(sent_v, held_v)
    rv.step(0)
    fv.step(6)
    for j in range(slots):
        rows = pl.ds(j * BLOCK, BLOCK)
        block = got_v[place[j]]
        v_s[rows, :] = block
        vt_s[:, rows] = block.T

    def backward(i, carry):
        for n, at_step in ((1, 3), (2, 5)):
            @pl.when(i == at_step)
            def _():
                rv.step(n)

        h = lax.rem(i, 2)
        cols = rows_at(i // 2, QB)
        band = rows_at(h, HEAD_DIM)
        att = dot(vt_s[band, :], p_s[h, :, cols]).astype(BF)
        att_t[band, cols] = att
        delta = jnp.sum(
            att.astype(F32) * datm[h, band, cols].astype(F32), axis=0, keepdims=True
        )
        dat = datm[h, :, cols]
        for c in range(chunks):
            rows = pl.ds(c * KC, KC)
            dp = dot(v_s[rows, :], dat)
            p_s[h, rows, cols] = (p_s[h, rows, cols].astype(F32) * (dp - delta)).astype(BF)
        dq_t[band, cols] = (dot(kt_s[band, :], p_s[h, :, cols]) * SCALE).astype(BF)
        return carry

    lax.fori_loop(0, steps, backward, 0)
    att_s[...] = att_t[...].T
    dq_s[...] = dq_t[...].T
    stores[0].start()
    at.step(0)
    contract(SCALE, qm)
    hand_out(sent_k, held_k)
    rk.step(0)
    rv.step(3)
    at.step(1)
    rk.step(1)
    rv.step(4)
    rv.step(5)
    rk.step(2)
    at.step(2)
    loads[5].wait()
    rv.step(6)
    rv.step(7)
    stores[2].start()
    rk.step(3)
    at.step(3)

    def mix(i, carry):
        rows = rows_at(i, QB)
        acc = None
        for g in range(2 * NX):
            part = dot(at_all[g, rows, :], w_cols[pl.ds(g * COLS, COLS), :])
            acc = part if acc is None else acc + part
        mixed_s[rows, :] = acc.astype(BF)
        return carry

    lax.fori_loop(0, tokens // QB, mix, 0)
    stores[1].start()
    rk.step(4)
    rk.step(5)
    fk.step(7)
    fv.step(7)
    og.step(4)
    at.step(4)
    rv.step(8)
    rk.step(6)
    rk.step(7)
    stores[3].start()
    rk.step(8)
    for store in stores:
        store.wait()


def layer(table, place, slot_of, q, k, v, w, og):
    tokens = q.shape[0]
    keys = place.shape[0] * BLOCK
    hbm = pl.BlockSpec(memory_space=pl.ANY)
    smem = pl.BlockSpec(memory_space=pltpu.SMEM)

    def vmem(*shape, dtype=BF):
        return pltpu.VMEM(shape, dtype)

    def bufs(cls):
        return [vmem(b, a, BLOCK, COLS) for a, b in cls.scratch]

    rows = jax.ShapeDtypeStruct((tokens, COLS), BF)
    cut = jax.ShapeDtypeStruct((NB, BLOCK, COLS), BF)
    return pl.pallas_call(
        layer_kernel,
        out_shape=(rows, rows, cut, cut),
        in_specs=[smem, smem, smem] + [hbm] * 5,
        out_specs=(hbm,) * 4,
        scratch_shapes=bufs(Fetch) + bufs(Fetch) + bufs(Return) + bufs(Return) + [
            vmem(NB, BLOCK, COLS),
            vmem(NB, BLOCK, COLS),
            vmem(tokens, COLS),
            vmem(tokens, COLS),
            vmem(COLS, w.shape[1]),
            vmem(w.shape[0], COLS),
            vmem(NY * NZ, BLOCK, COLS),
            vmem(NY * NZ, BLOCK, COLS),
            vmem(2 * NX, tokens, COLS),
            vmem(2 * NX, tokens, COLS),
            vmem(NY - 1, NZ, BLOCK, COLS),
            vmem(NY - 1, NZ, BLOCK, COLS),
            vmem(NY, NZ, BLOCK, COLS),
            vmem(NY, NZ, BLOCK, COLS),
            vmem(2, tokens, COLS),
            vmem(2, COLS, tokens),
            vmem(2, tokens, COLS),
            vmem(2, COLS, tokens),
            vmem(keys, COLS),
            vmem(COLS, keys),
            vmem(keys, COLS),
            vmem(COLS, keys),
            vmem(keys, QB, dtype=F32),
            vmem(2, keys, tokens),
            vmem(COLS, tokens),
            vmem(COLS, tokens),
            vmem(keys // BLOCK, BLOCK, COLS),
            vmem(tokens, COLS),
            vmem(tokens, COLS),
            vmem(tokens, COLS),
            vmem(NB, BLOCK, COLS),
            vmem(NB, BLOCK, COLS),
            pltpu.SemaphoreType.DMA((136,)),
            pltpu.SemaphoreType.DMA((136,)),
            pltpu.SemaphoreType.DMA((10,)),
        ],
        compiler_params=pltpu.CompilerParams(
            collective_id=0, has_side_effects=True, vmem_limit_bytes=56 * 2**20
        ),
        name="layer",
    )(table, place, slot_of, q, k, v, w, og)


def routes(source_view, source_block):
    view = lax.axis_index("view")
    views = jnp.arange(NZ * NY, dtype=jnp.int32)
    same = source_view[:, :, None] == views[None, None, :]
    table = jnp.max(jnp.where(same, source_block[:, :, None], -1), axis=1).reshape(-1)
    own = lax.dynamic_index_in_dim(source_view, view, 0, keepdims=False)
    dz = lax.rem(view // NY - own // NY + NZ, NZ)
    dy = lax.rem(lax.rem(view, NY) - lax.rem(own, NY) + NY, NY)
    place = dy * NZ + jnp.where(dz == 0, 0, jnp.where(dz <= 4, 2 * dz - 1, 16 - 2 * dz))
    order = jnp.arange(own.shape[0], dtype=jnp.int32)
    slot_of = jnp.max(jnp.where(place[None, :] == views[:, None], order[None, :], 0), axis=1)
    return table, place, slot_of


def body(query_rows, key_rows, value_rows, out_weight, out_grad, source_view, source_block):
    cut = (NB, BLOCK, COLS)
    table, place, slot_of = routes(source_view, source_block)
    mixed, dq, kg, vg = layer(
        table, place, slot_of,
        query_rows, key_rows.reshape(cut), value_rows.reshape(cut), out_weight, out_grad,
    )
    return mixed, dq, kg.reshape(query_rows.shape), vg.reshape(query_rows.shape)


def solution(mesh):
    spread = P("view", "head")
    return jax.shard_map(
        body,
        mesh=mesh,
        in_specs=(spread, spread, spread, P(), spread, P(), P()),
        out_specs=(spread, spread, spread, spread),
        check_vma=False,
    )
```

```python
import jax
import jax.numpy as jnp
from jax import lax
from jax.experimental import pallas as pl
from jax.experimental.pallas import tpu as pltpu
from jax.sharding import PartitionSpec as P

HEAD_DIM = 64
BLOCK = 128
COLS = 2 * HEAD_DIM
SCALE = HEAD_DIM ** -0.5
LOG2E = 1.4426950408889634
QB = 256
KC = 256
BF = jnp.bfloat16
F32 = jnp.float32


def dot(a, b):
    return jnp.dot(a, b, preferred_element_type=jnp.float32)


MESH = pl.DeviceIdType.MESH
NZ, NY, NX = 8, 4, 4
NB = 8


class Copies:
    def __init__(self, send, recv):
        self.send, self.recv, self.n = send, recv, 0

    def make(self, src, dst, device):
        i = self.n
        self.n += 1
        return pltpu.make_async_remote_copy(
            src_ref=src,
            dst_ref=dst,
            send_sem=self.send.at[i],
            recv_sem=self.recv.at[i],
            device_id=device,
            device_id_type=MESH,
        )


class Place:
    def __init__(self):
        view = lax.axis_index("view")
        head = lax.axis_index("head")
        self.view, self.head = view, head
        self.z, self.y = view // NY, lax.rem(view, NY)
        self.x, self.c = head // 2, lax.rem(head, 2)

    def zplus(self, d):
        return lax.rem(self.z + d + NZ, NZ)

    def yplus(self, k):
        return lax.rem(self.y + k + NY, NY)

    def at_z(self, d):
        return {"view": self.zplus(d) * NY + self.y}

    def at_y(self, k):
        return {"view": self.z * NY + self.yplus(k)}

    def at_x(self, d):
        return {"head": lax.rem(self.x + d + NX, NX) * 2 + self.c}

    def partner(self):
        return {"head": self.x * 2 + 1 - self.c}

    def pick(self, table, dz, k, sz):
        taker = self.zplus(dz) * NY + self.yplus(k)
        return table[self.zplus(sz) * NY + self.y, taker]

    def pick_abs(self, table, dz, yd, sz):
        taker = self.zplus(dz) * NY + yd
        return table[self.zplus(sz) * NY + self.y, taker]


def greet(here, zy=True, x=True):
    barrier = pltpu.get_barrier_semaphore()
    peers = []
    if zy:
        peers += [here.at_z(1), here.at_z(-1), here.at_y(1), here.at_y(2), here.at_y(3)]
    if x:
        peers += [here.at_x(1), here.at_x(-1), here.partner()]
    for peer in peers:
        pl.semaphore_signal(barrier, inc=1, device_id=peer, device_id_type=MESH)
    pl.semaphore_wait(barrier, len(peers))


class Gather:
    def __init__(self, here, copies, own, full):
        rows = own.shape[0]
        half = rows // 2
        x, c = here.x, here.c
        me = here.head
        left = lax.rem(x + NX - 1, NX) * 2 + c
        right = lax.rem(x + 1, NX) * 2 + c
        far = lax.rem(x + 2, NX) * 2 + c
        lo, hi = pl.ds(0, half), pl.ds(half, half)
        self.own, self.full, self.me = own, full, me
        mk = copies.make
        self.first = [
            mk(own, full.at[me], here.at_x(1)),
            mk(own, full.at[me], here.at_x(-1)),
        ]
        self.second = [
            mk(full.at[left, lo], full.at[left, lo], here.at_x(1)),
            mk(full.at[right, hi], full.at[right, hi], here.at_x(-1)),
        ]
        self.across = [
            mk(own, full.at[me], here.partner()),
            mk(full.at[left], full.at[left], here.partner()),
            mk(full.at[right], full.at[right], here.partner()),
            mk(full.at[far], full.at[far], here.partner()),
        ]

    def step(self, n):
        if n == 0:
            for copy in self.first:
                copy.start()
            self.across[0].start()
            self.full[self.me] = self.own[...]
        if n == 1:
            for copy in self.first:
                copy.wait_recv()
            for copy in self.second:
                copy.start()
            self.across[1].start()
            self.across[2].start()
        if n == 2:
            for copy in self.second:
                copy.wait_recv()
            self.across[3].start()
        if n == 3:
            for copy in self.across:
                copy.wait_recv()
        if n == 4:
            for copy in self.first + self.second + self.across:
                copy.wait_send()


FETCH_PIECES = ((0, 1), (1, 3), (3, 5), (5, 7), (7, 8))


class Fetch:
    scratch = ((8, 2), (8, 2), (6, 2), (2, 2), (6, 2), (NB, 3))

    def __init__(self, here, copies, table, own, got, bufs):
        self.here, self.table, self.own, self.got = here, table, own, got
        one, two, three, four, fwd, stage = bufs
        self.one, self.two, self.three, self.four = one, two, three, four
        self.fwd, self.stage = fwd, stage
        mk = copies.make
        ways = (here.at_z(1), here.at_z(-1))
        h = NB // 2
        self.c1, self.c2, self.c3, self.c4 = [], [], [], []
        for part in range(2):
            for s, way in enumerate(ways):
                self.c1.append(mk(own.at[pl.ds(part * h, h)], one.at[s, pl.ds(part * h, h)], way))
        for part in range(2):
            for s, way in enumerate(ways):
                self.c2.append(
                    mk(one.at[s, pl.ds(part * h, h)], two.at[s, pl.ds(part * h, h)], way)
                )
        for s, way in enumerate(ways):
            self.c3.append(mk(fwd.at[s], three.at[s], way))
        for s, way in enumerate(ways):
            self.c4.append(mk(three.at[s, pl.ds(4, 2)], four.at[s], way))
        self.cy = []
        for a, b in FETCH_PIECES:
            self.cy.append(
                [
                    mk(
                        stage.at[k - 1, pl.ds(a, b - a)],
                        got.at[pl.ds(k * NZ + a, b - a)],
                        here.at_y(k),
                    )
                    for k in (2, 1, 3)
                ]
            )

    def put(self, k, e, value):
        if k == 0:
            self.got[e] = value
        else:
            self.stage[k - 1, e] = value

    def select(self, src, k, sz):
        return src[jnp.maximum(self.here.pick(self.table, 0, k, sz), 0)]

    def start_y(self, piece):
        for copy in self.cy[piece]:
            copy.start()

    def offer(self, part):
        for copy in self.c1[part * 2 : part * 2 + 2]:
            copy.start()

    def step(self, n):
        here, table = self.here, self.table
        if n == 0:
            for k in range(NY):
                self.put(k, 0, self.select(self.own, k, 0))
            self.start_y(0)
        if n in (1, 2):
            part = n - 1
            for s in range(2):
                self.c1[part * 2 + s].wait_recv()
                self.c2[part * 2 + s].start()
        if n == 2:
            for k in range(NY):
                self.put(k, 1, self.select(self.one.at[0], k, -1))
                self.put(k, 2, self.select(self.one.at[1], k, 1))
            self.start_y(1)
        if n == 3:
            for copy in self.c2:
                copy.wait_recv()
            for s, d in ((0, 1), (1, -1)):
                src = self.two.at[s]
                for yd in range(4):
                    b = jnp.maximum(here.pick_abs(table, d, yd, -2 * d), 0)
                    self.fwd[s, yd] = src[b]
                for i in range(2):
                    b = jnp.maximum(here.pick_abs(table, 2 * d, 2 * s + i, -2 * d), 0)
                    self.fwd[s, 4 + i] = src[b]
            for k in range(NY):
                self.put(k, 3, self.select(self.two.at[0], k, -2))
                self.put(k, 4, self.select(self.two.at[1], k, 2))
            for copy in self.c3:
                copy.start()
            self.start_y(2)
        if n == 4:
            for s in range(2):
                self.c3[s].wait_recv()
                self.c4[s].start()
            for k in range(NY):
                yd = here.yplus(k)
                self.put(k, 5, self.three[0, yd])
                self.put(k, 6, self.three[1, yd])
            self.start_y(3)
        if n == 5:
            for copy in self.c4:
                copy.wait_recv()
            for k in range(NY):
                yd = here.yplus(k)
                low = lax.rem(yd, 2)
                self.put(k, 7, jnp.where(yd < 2, self.four[0, low], self.four[1, low]))
            self.start_y(4)
        if n == 6:
            for piece in self.cy:
                for copy in piece:
                    copy.wait_recv()
        if n == 7:
            for copy in self.c1 + self.c2 + self.c3 + self.c4:
                copy.wait_send()
            for piece in self.cy:
                for copy in piece:
                    copy.wait_send()


RETURN_PIECES = ((7, 8), (5, 7), (3, 5), (1, 3), (0, 1))


class Return:
    scratch = ((2, 2), (6, 2), (8, 2), (8, 2), (8, 2), (8, 2))

    def __init__(self, here, copies, table, sent, held, out, bufs):
        self.here, self.table, self.held, self.out = here, table, held, out
        four, three, two, one, out2, out1 = bufs
        self.four, self.three, self.two, self.one = four, three, two, one
        self.out2, self.out1 = out2, out1
        mk = copies.make
        ways = (here.at_z(-1), here.at_z(1))
        h = NB // 2
        self.cy = []
        for a, b in RETURN_PIECES:
            self.cy.append(
                [
                    mk(sent.at[k - 1, pl.ds(a, b - a)], held.at[k, pl.ds(a, b - a)], here.at_y(-k))
                    for k in (2, 1, 3)
                ]
            )
        self.c4, self.c3, self.c2, self.c1 = [], [], [], []
        for s, way in enumerate(ways):
            for i in range(2):
                k = lax.rem(2 * s + i + NY - here.y, NY)
                self.c4.append(mk(held.at[k, 7], four.at[s, i], way))
        for s, way in enumerate(ways):
            self.c3.append(mk(held.at[:, 5 + s], three.at[s, pl.ds(0, 4)], way))
        for s, way in enumerate(ways):
            self.c3.append(mk(four.at[s], three.at[s, pl.ds(4, 2)], way))
        for part in range(2):
            for s, way in enumerate(ways):
                self.c2.append(
                    mk(out2.at[s, pl.ds(part * h, h)], two.at[s, pl.ds(part * h, h)], way)
                )
        for part in range(2):
            for s, way in enumerate(ways):
                self.c1.append(
                    mk(out1.at[s, pl.ds(part * h, h)], one.at[s, pl.ds(part * h, h)], way)
                )

    def start_y(self, piece):
        for copy in self.cy[piece]:
            copy.start()

    def wait_y(self, piece):
        for copy in self.cy[piece]:
            copy.wait_recv()

    @staticmethod
    def total(b, bases, terms):
        acc = None
        for value in bases:
            value = value.astype(jnp.float32)
            acc = value if acc is None else acc + value
        for pick, ref in terms:
            value = ref[...].astype(jnp.float32)
            value = jnp.where(pick == b, value, jnp.zeros_like(value))
            acc = value if acc is None else acc + value
        return acc.astype(jnp.bfloat16)

    def here_terms(self, e, sz):
        return [
            (self.here.pick(self.table, 0, k, sz), self.held.at[k, e]) for k in range(NY)
        ]

    def step(self, n):
        here, table = self.here, self.table
        h = NB // 2
        if n == 1:
            self.wait_y(0)
            for copy in self.c4:
                copy.start()
        if n == 2:
            self.wait_y(1)
            for copy in self.c3[:2]:
                copy.start()
        if n == 3:
            for copy in self.c4:
                copy.wait_recv()
            for copy in self.c3[2:]:
                copy.start()
        if n == 4:
            self.wait_y(2)
            for copy in self.c3:
                copy.wait_recv()
            for part in range(2):
                for s, d in ((0, 1), (1, -1)):
                    terms = self.here_terms(3 + s, -2 * d)
                    for k in range(4):
                        terms.append((here.pick(table, d, k, -2 * d), self.three.at[s, k]))
                    for i in range(2):
                        pick = here.pick_abs(table, 2 * d, 2 * s + i, -2 * d)
                        terms.append((pick, self.three.at[s, 4 + i]))
                    for b in range(part * h, part * h + h):
                        self.out2[s, b] = self.total(b, [], terms)
                for s in range(2):
                    self.c2[part * 2 + s].start()
        if n in (5, 6):
            part = n - 5
            if n == 5:
                self.wait_y(3)
            for s, d in ((0, 1), (1, -1)):
                self.c2[part * 2 + s].wait_recv()
                terms = self.here_terms(1 + s, -d)
                for b in range(part * h, part * h + h):
                    self.out1[s, b] = self.total(b, [self.two[s, b]], terms)
            for s in range(2):
                self.c1[part * 2 + s].start()
        if n in (7, 8):
            part = n - 7
            if n == 7:
                self.wait_y(4)
            for s in range(2):
                self.c1[part * 2 + s].wait_recv()
            terms = self.here_terms(0, 0)
            for b in range(part * h, part * h + h):
                self.out[b] = self.total(b, [self.one[0, b], self.one[1, b]], terms)
        if n == 9:
            for copy in self.c4 + self.c3 + self.c2 + self.c1:
                copy.wait_send()
            for piece in self.cy:
                for copy in piece:
                    copy.wait_send()


def rows_at(i, size):
    return pl.ds(pl.multiple_of(i * size, size), size)


def routes(view, sv_ref, sb_ref, pack_ref):
    slots, views = sv_ref.shape
    sv, sb = sv_ref[...], sb_ref[...]
    wide = (views, views)
    source = lax.broadcasted_iota(jnp.int32, wide, 0)
    table = jnp.full(wide, -1, jnp.int32)
    for j in range(slots):
        same = jnp.broadcast_to(sv[j : j + 1, :], wide) == source
        table = jnp.where(same, jnp.broadcast_to(sb[j : j + 1, :], wide), table)
    pack_ref[0:views, 0:views] = table
    lanes = lax.broadcasted_iota(jnp.int32, sv.shape, 1)
    own = jnp.sum(jnp.where(lanes == view, sv, 0), axis=1, keepdims=True)
    dz = (view // NY - own // NY + NZ) & (NZ - 1)
    dy = ((view & (NY - 1)) - (own & (NY - 1)) + NY) & (NY - 1)
    near = jnp.where(dz == 0, 0, jnp.where(dz <= NZ // 2, 2 * dz - 1, 2 * NZ - 2 * dz))
    place = jnp.broadcast_to(dy * NZ + near, (slots, BLOCK))
    pack_ref[views : views + slots, :] = place
    order = lax.broadcasted_iota(jnp.int32, place.shape, 0)
    spot = lax.broadcasted_iota(jnp.int32, place.shape, 1)
    slot_of = jnp.max(jnp.where(place == spot, order, 0), axis=0, keepdims=True)
    pack_ref[views + slots : views + slots + 8, :] = jnp.broadcast_to(slot_of, (8, BLOCK))


def layer_kernel(
    sv_ref, sb_ref, q_hbm, k_hbm, v_hbm, w_hbm, og_hbm,
    mixed_ref, dq_ref, ok_ref, ov_ref,
    *scratch,
):
    fbk, fbv, rbk, rbv = scratch[:6], scratch[6:12], scratch[12:18], scratch[18:24]
    (
        k_own, v_own, og_own, q_s, w_rows, w_cols,
        got_k, got_v, og_all, at_all, sent_k, sent_v, held_k, held_v,
        qm, qtm, dam, datm, k_s, kt_s, v_s, vt_s, s_s, p_s,
        att_t, dq_t, grad_s, att_s, inv_s, delta_s, pack_v, pack,
        send, recv, local,
    ) = scratch[24:]
    here = Place()
    copies = Copies(send, recv)
    slots, views = sv_ref.shape
    keys = slots * BLOCK
    tokens = q_s.shape[0]
    chunks = keys // KC
    mine = pl.ds(pl.multiple_of(here.head * COLS, COLS), COLS)

    loads = [
        pltpu.make_async_copy(src, dst, local.at[i])
        for i, (src, dst) in enumerate(
            (
                (k_hbm, k_own),
                (og_hbm, og_own),
                (v_hbm, v_own),
                (q_hbm, q_s),
                (w_hbm.at[mine, :], w_rows),
                (w_hbm.at[:, mine], w_cols),
            )
        )
    ]
    for load in loads:
        load.start()
    tables = pltpu.make_async_copy(pack_v, pack, local.at[len(loads)])
    routes(here.view, sv_ref, sb_ref, pack_v)
    tables.start()

    og = Gather(here, copies, og_own, og_all)
    fk = Fetch(here, copies, pack, k_own, got_k, fbk)
    fv = Fetch(here, copies, pack, v_own, got_v, fbv)
    at = Gather(here, copies, att_s, at_all)
    rk = Return(here, copies, pack, sent_k, held_k, ok_ref, rbk)
    rv = Return(here, copies, pack, sent_v, held_v, ov_ref, rbv)

    greet(here)
    loads[0].wait()
    fk.offer(0)
    fk.offer(1)
    loads[1].wait()
    og.step(0)
    tables.wait()
    fk.step(0)
    loads[2].wait()
    fv.step(0)
    loads[3].wait()
    q = q_s[...]
    lane = lax.broadcasted_iota(jnp.int32, q.shape, 1) // HEAD_DIM
    for h in range(2):
        part = jnp.where(lane == h, q, jnp.zeros_like(q))
        qm[h] = part
        qtm[h] = part.T
    fk.step(1)
    fk.step(2)
    fv.offer(0)
    og.step(1)
    fk.step(3)
    fv.offer(1)
    og.step(2)
    loads[4].wait()
    og.step(3)

    def project(i, carry):
        rows = rows_at(i, QB)
        acc = None
        for g in range(2 * NX):
            part = lax.dot_general(
                og_all[g, rows, :],
                w_rows[:, pl.ds(g * COLS, COLS)],
                (((1,), (1,)), ((), ())),
                preferred_element_type=jnp.float32,
            )
            acc = part if acc is None else acc + part
        da = acc.astype(BF)
        half = lax.broadcasted_iota(jnp.int32, da.shape, 1) // HEAD_DIM
        for h in range(2):
            part = jnp.where(half == h, da, jnp.zeros_like(da))
            dam[h, rows, :] = part
            datm[h, :, rows] = part.T
        return carry

    lax.fori_loop(0, tokens // QB, project, 0)
    fk.step(4)
    fv.step(1)
    fk.step(5)
    fv.step(2)
    fk.step(6)
    for j in range(slots):
        k_s[pl.ds(j * BLOCK, BLOCK), :] = got_k[pack[views + j, 0]]

    steps = 2 * (tokens // QB)

    def forward(i, carry):
        @pl.when(i == 2)
        def _():
            fv.step(3)

        h = lax.rem(i, 2)
        cols = rows_at(i // 2, QB)
        qt = qtm[h, :, cols]
        top = None
        for c in range(chunks):
            rows = pl.ds(c * KC, KC)
            s = dot(k_s[rows, :], qt)
            s_s[rows, :] = s
            m = jnp.max(s, axis=0, keepdims=True)
            top = m if top is None else jnp.maximum(top, m)
        shift = top * (SCALE * LOG2E)
        total = jnp.zeros((1, QB), F32)
        for c in range(chunks):
            rows = pl.ds(c * KC, KC)
            e = jnp.exp2(s_s[rows, :] * (SCALE * LOG2E) - shift)
            p_s[h, rows, cols] = e.astype(BF)
            total = total + jnp.sum(e, axis=0, keepdims=True)
        inv = jnp.broadcast_to(1.0 / total, (8, QB))
        inv_s[h, :, cols] = inv
        down = inv.T[:, 0:1]
        dam[h, cols, :] = (dam[h, cols, :].astype(F32) * down).astype(BF)
        qm[h, cols, :] = (qm[h, cols, :].astype(F32) * down).astype(BF)
        return carry

    lax.fori_loop(0, steps, forward, 0)

    def grads(c, rows, right, scale):
        g = dot(p_s[0, rows, :], right[0]) + dot(p_s[1, rows, :], right[1])
        if scale is not None:
            g = g * scale
        g = g.astype(BF)
        for b in range(KC // BLOCK):
            grad_s[c * (KC // BLOCK) + b] = g[b * BLOCK : (b + 1) * BLOCK, :]

    def value_grads(c, carry):
        grads(c, rows_at(c, KC), dam, None)
        return carry

    def hand_out(sent, held):
        for e in range(NZ):
            held[0, e] = grad_s[pack[views + slots, e]]
        for k in range(1, NY):
            for e in range(NZ):
                sent[k - 1, e] = grad_s[pack[views + slots, k * NZ + e]]

    lax.fori_loop(0, chunks, value_grads, 0)
    fv.step(4)
    hand_out(sent_v, held_v)
    rv.start_y(0)
    fv.step(5)
    rv.start_y(1)
    rv.step(1)
    fv.step(6)
    rv.start_y(2)
    rv.start_y(3)
    rv.start_y(4)
    for j in range(slots):
        rows = pl.ds(j * BLOCK, BLOCK)
        block = got_v[pack[views + j, 0]]
        v_s[rows, :] = block
        vt_s[:, rows] = block.T

    def attend(i, carry):
        h = lax.rem(i, 2)
        cols = rows_at(i // 2, QB)
        band = rows_at(h, HEAD_DIM)
        att = dot(vt_s[band, :], p_s[h, :, cols]) * inv_s[h, 0:1, cols]
        att = att.astype(BF)
        att_t[band, cols] = att
        delta = jnp.sum(
            att.astype(F32) * datm[h, band, cols].astype(F32), axis=0, keepdims=True
        )
        delta_s[h, :, cols] = jnp.broadcast_to(delta, (8, QB))
        return carry

    lax.fori_loop(0, steps, attend, 0)
    att_s[...] = att_t[...].T
    at.step(0)

    def key_grads(c, carry):
        @pl.when(c == 1)
        def _():
            rv.step(2)
            rv.step(3)

        @pl.when(c == 6)
        def _():
            at.step(1)

        rows = rows_at(c, KC)
        right = v_s[rows, :]
        for h in range(2):
            for i in range(tokens // QB):
                cols = pl.ds(i * QB, QB)
                dp = dot(right, datm[h, :, cols]) - delta_s[h, 0:1, cols]
                p_s[h, rows, cols] = (p_s[h, rows, cols].astype(F32) * dp).astype(BF)
        grads(c, rows, qm, SCALE)
        return carry

    lax.fori_loop(0, chunks, key_grads, 0)
    hand_out(sent_k, held_k)
    rk.start_y(0)
    rk.start_y(1)
    rv.step(4)
    rk.start_y(2)
    rk.start_y(3)
    rk.start_y(4)
    for j in range(slots):
        kt_s[:, pl.ds(j * BLOCK, BLOCK)] = k_s[pl.ds(j * BLOCK, BLOCK), :].T

    def query_grads(i, carry):
        @pl.when(i == 4)
        def _():
            rk.step(1)

        h = lax.rem(i, 2)
        cols = rows_at(i // 2, QB)
        band = rows_at(h, HEAD_DIM)
        dq = dot(kt_s[band, :], p_s[h, :, cols]) * (inv_s[h, 0:1, cols] * SCALE)
        dq_t[band, cols] = dq.astype(BF)
        return carry

    lax.fori_loop(0, steps, query_grads, 0)
    rk.step(2)
    rv.step(5)
    at.step(2)
    rk.step(3)
    rv.step(6)
    dq_ref[...] = dq_t[...].T
    rk.step(4)
    loads[5].wait()
    at.step(3)

    def mix(i, carry):
        rows = rows_at(i, QB)
        acc = None
        for g in range(2 * NX):
            part = dot(at_all[g, rows, :], w_cols[pl.ds(g * COLS, COLS), :])
            acc = part if acc is None else acc + part
        mixed_ref[rows, :] = acc.astype(BF)
        return carry

    rk.step(5)
    rv.step(7)
    rv.step(8)
    rk.step(6)
    lax.fori_loop(0, tokens // QB, mix, 0)
    fk.step(7)
    fv.step(7)
    og.step(4)
    at.step(4)
    rv.step(9)
    rk.step(7)
    rk.step(8)
    rk.step(9)


def layer(sv, sb, q, k, v, w, og):
    tokens = q.shape[0]
    slots, views = sv.shape
    keys = slots * BLOCK
    hbm = pl.BlockSpec(memory_space=pl.ANY)
    vm = pl.BlockSpec(memory_space=pltpu.VMEM)

    def vmem(*shape, dtype=BF):
        return pltpu.VMEM(shape, dtype)

    def bufs(cls):
        return [vmem(b, a, BLOCK, COLS) for a, b in cls.scratch]

    rows = jax.ShapeDtypeStruct((tokens, COLS), BF)
    cut = jax.ShapeDtypeStruct((NB, BLOCK, COLS), BF)
    return pl.pallas_call(
        layer_kernel,
        out_shape=(rows, rows, cut, cut),
        in_specs=[vm, vm] + [hbm] * 5,
        out_specs=(vm,) * 4,
        scratch_shapes=bufs(Fetch) + bufs(Fetch) + bufs(Return) + bufs(Return) + [
            vmem(NB, BLOCK, COLS),
            vmem(NB, BLOCK, COLS),
            vmem(tokens, COLS),
            vmem(tokens, COLS),
            vmem(COLS, w.shape[1]),
            vmem(w.shape[0], COLS),
            vmem(NY * NZ, BLOCK, COLS),
            vmem(NY * NZ, BLOCK, COLS),
            vmem(2 * NX, tokens, COLS),
            vmem(2 * NX, tokens, COLS),
            vmem(NY - 1, NZ, BLOCK, COLS),
            vmem(NY - 1, NZ, BLOCK, COLS),
            vmem(NY, NZ, BLOCK, COLS),
            vmem(NY, NZ, BLOCK, COLS),
            vmem(2, tokens, COLS),
            vmem(2, COLS, tokens),
            vmem(2, tokens, COLS),
            vmem(2, COLS, tokens),
            vmem(keys, COLS),
            vmem(COLS, keys),
            vmem(keys, COLS),
            vmem(COLS, keys),
            vmem(keys, QB, dtype=F32),
            vmem(2, keys, tokens),
            vmem(COLS, tokens),
            vmem(COLS, tokens),
            vmem(slots, BLOCK, COLS),
            vmem(tokens, COLS),
            vmem(2, 8, tokens, dtype=F32),
            vmem(2, 8, tokens, dtype=F32),
            vmem(views + slots + 8, BLOCK, dtype=jnp.int32),
            pltpu.SMEM((views + slots + 8, BLOCK), jnp.int32),
            pltpu.SemaphoreType.DMA((136,)),
            pltpu.SemaphoreType.DMA((136,)),
            pltpu.SemaphoreType.DMA((8,)),
        ],
        compiler_params=pltpu.CompilerParams(
            collective_id=0, has_side_effects=True, vmem_limit_bytes=56 * 2**20
        ),
        name="layer",
    )(sv, sb, q, k, v, w, og)


def finish_kernel(*refs):
    sems = refs[-1]
    n = (len(refs) - 1) // 2
    moves = [pltpu.make_async_copy(refs[i], refs[n + i], sems.at[i]) for i in range(n)]
    for move in moves:
        move.start()
    for move in moves:
        move.wait()


def finish(*arrays):
    vm = pl.BlockSpec(memory_space=pltpu.VMEM)
    hbm = pl.BlockSpec(memory_space=pl.ANY)
    return pl.pallas_call(
        finish_kernel,
        out_shape=tuple(jax.ShapeDtypeStruct(a.shape, a.dtype) for a in arrays),
        in_specs=[vm] * len(arrays),
        out_specs=(hbm,) * len(arrays),
        scratch_shapes=[pltpu.SemaphoreType.DMA((len(arrays),))],
        name="finish",
    )(*arrays)


def body(query_rows, key_rows, value_rows, out_weight, out_grad, source_view, source_block):
    cut = (NB, BLOCK, COLS)
    mixed, dq, kg, vg = finish(*layer(
        source_view.T, source_block.T,
        query_rows, key_rows.reshape(cut), value_rows.reshape(cut), out_weight, out_grad,
    ))
    return mixed, dq, kg.reshape(query_rows.shape), vg.reshape(query_rows.shape)


def solution(mesh):
    spread = P("view", "head")
    return jax.shard_map(
        body,
        mesh=mesh,
        in_specs=(spread, spread, spread, P(), spread, P(), P()),
        out_specs=(spread, spread, spread, spread),
        check_vma=False,
    )
```

```python
import jax
import jax.numpy as jnp
from jax import lax
from jax.experimental import pallas as pl
from jax.experimental.pallas import tpu as pltpu
from jax.sharding import PartitionSpec as P

HEAD_DIM = 64
BLOCK = 128
COLS = 2 * HEAD_DIM
SCALE = HEAD_DIM ** -0.5
LOG2E = 1.4426950408889634
QB = 256
KC = 256
BF = jnp.bfloat16
F32 = jnp.float32


def dot(a, b):
    return jnp.dot(a, b, preferred_element_type=jnp.float32)


MESH = pl.DeviceIdType.MESH
NZ, NY, NX = 8, 4, 4
NB = 8


class Copies:
    def __init__(self, send, recv):
        self.send, self.recv, self.n = send, recv, 0

    def make(self, src, dst, device):
        i = self.n
        self.n += 1
        return pltpu.make_async_remote_copy(
            src_ref=src,
            dst_ref=dst,
            send_sem=self.send.at[i],
            recv_sem=self.recv.at[i],
            device_id=device,
            device_id_type=MESH,
        )


class Place:
    def __init__(self):
        view = lax.axis_index("view")
        head = lax.axis_index("head")
        self.view, self.head = view, head
        self.z, self.y = view // NY, lax.rem(view, NY)
        self.x, self.c = head // 2, lax.rem(head, 2)

    def zplus(self, d):
        return lax.rem(self.z + d + NZ, NZ)

    def yplus(self, k):
        return lax.rem(self.y + k + NY, NY)

    def at_z(self, d):
        return {"view": self.zplus(d) * NY + self.y}

    def at_y(self, k):
        return {"view": self.z * NY + self.yplus(k)}

    def at_x(self, d):
        return {"head": lax.rem(self.x + d + NX, NX) * 2 + self.c}

    def partner(self):
        return {"head": self.x * 2 + 1 - self.c}

    def pick(self, table, dz, k, sz):
        taker = self.zplus(dz) * NY + self.yplus(k)
        return table[self.zplus(sz) * NY + self.y, taker]

    def pick_abs(self, table, dz, yd, sz):
        taker = self.zplus(dz) * NY + yd
        return table[self.zplus(sz) * NY + self.y, taker]


def greet(here):
    barrier = pltpu.get_barrier_semaphore()
    peers = [here.at_z(1), here.at_z(-1), here.at_y(1), here.at_y(2), here.at_y(3)]
    peers += [here.at_x(1), here.at_x(-1), here.partner()]
    for peer in peers:
        pl.semaphore_signal(barrier, inc=1, device_id=peer, device_id_type=MESH)
    return lambda: pl.semaphore_wait(barrier, len(peers))


class Gather:
    def __init__(self, here, copies, own, full):
        rows = own.shape[0]
        half = rows // 2
        x, c = here.x, here.c
        me = here.head
        left = lax.rem(x + NX - 1, NX) * 2 + c
        right = lax.rem(x + 1, NX) * 2 + c
        far = lax.rem(x + 2, NX) * 2 + c
        lo, hi = pl.ds(0, half), pl.ds(half, half)
        self.own, self.full, self.me = own, full, me
        mk = copies.make
        self.first = [
            mk(own, full.at[me], here.at_x(1)),
            mk(own, full.at[me], here.at_x(-1)),
        ]
        self.second = [
            mk(full.at[left, lo], full.at[left, lo], here.at_x(1)),
            mk(full.at[right, hi], full.at[right, hi], here.at_x(-1)),
        ]
        self.across = [
            mk(own, full.at[me], here.partner()),
            mk(full.at[left], full.at[left], here.partner()),
            mk(full.at[right], full.at[right], here.partner()),
            mk(full.at[far], full.at[far], here.partner()),
        ]

    def step(self, n):
        if n == 0:
            for copy in self.first:
                copy.start()
            self.across[0].start()
            self.full[self.me] = self.own[...]
        if n == 1:
            for copy in self.first:
                copy.wait_recv()
            for copy in self.second:
                copy.start()
            self.across[1].start()
            self.across[2].start()
        if n == 2:
            for copy in self.second:
                copy.wait_recv()
            self.across[3].start()
        if n == 3:
            for copy in self.across:
                copy.wait_recv()
        if n == 4:
            for copy in self.first + self.second + self.across:
                copy.wait_send()


FETCH_PIECES = ((0, 1), (1, 3), (3, 5), (5, 7), (7, 8))


class Fetch:
    scratch = ((8, 2), (8, 2), (6, 2), (2, 2), (6, 2), (NB, 3))

    def __init__(self, here, copies, table, own, got, bufs):
        self.here, self.table, self.own, self.got = here, table, own, got
        one, two, three, four, fwd, stage = bufs
        self.one, self.two, self.three, self.four = one, two, three, four
        self.fwd, self.stage = fwd, stage
        mk = copies.make
        ways = (here.at_z(1), here.at_z(-1))
        h = NB // 2
        self.c1, self.c2, self.c3, self.c4 = [], [], [], []
        for part in range(2):
            for s, way in enumerate(ways):
                self.c1.append(mk(own.at[pl.ds(part * h, h)], one.at[s, pl.ds(part * h, h)], way))
        for part in range(2):
            for s, way in enumerate(ways):
                self.c2.append(
                    mk(one.at[s, pl.ds(part * h, h)], two.at[s, pl.ds(part * h, h)], way)
                )
        for a, size in ((4, 2), (0, 4)):
            for s, way in enumerate(ways):
                self.c3.append(mk(fwd.at[s, pl.ds(a, size)], three.at[s, pl.ds(a, size)], way))
        for s, way in enumerate(ways):
            self.c4.append(mk(three.at[s, pl.ds(4, 2)], four.at[s], way))
        self.cy = []
        for a, b in FETCH_PIECES:
            self.cy.append(
                [
                    mk(
                        stage.at[k - 1, pl.ds(a, b - a)],
                        got.at[pl.ds(k * NZ + a, b - a)],
                        here.at_y(k),
                    )
                    for k in (2, 1, 3)
                ]
            )

    def put(self, k, e, value):
        if k == 0:
            self.got[e] = value
        else:
            self.stage[k - 1, e] = value

    def select(self, src, k, sz):
        return src[jnp.maximum(self.here.pick(self.table, 0, k, sz), 0)]

    def start_y(self, piece):
        for copy in self.cy[piece]:
            copy.start()

    def offer(self, part):
        for copy in self.c1[part * 2 : part * 2 + 2]:
            copy.start()

    def step(self, n):
        here, table = self.here, self.table
        if n == 0:
            for k in range(NY):
                self.put(k, 0, self.select(self.own, k, 0))
            self.start_y(0)
        if n in (1, 2):
            part = n - 1
            for s in range(2):
                self.c1[part * 2 + s].wait_recv()
                self.c2[part * 2 + s].start()
        if n == 2:
            for k in range(NY):
                self.put(k, 1, self.select(self.one.at[0], k, -1))
                self.put(k, 2, self.select(self.one.at[1], k, 1))
            self.start_y(1)
        if n == 3:
            for copy in self.c2:
                copy.wait_recv()
            for s, d in ((0, 1), (1, -1)):
                src = self.two.at[s]
                for yd in range(4):
                    b = jnp.maximum(here.pick_abs(table, d, yd, -2 * d), 0)
                    self.fwd[s, yd] = src[b]
                for i in range(2):
                    b = jnp.maximum(here.pick_abs(table, 2 * d, 2 * s + i, -2 * d), 0)
                    self.fwd[s, 4 + i] = src[b]
            for k in range(NY):
                self.put(k, 3, self.select(self.two.at[0], k, -2))
                self.put(k, 4, self.select(self.two.at[1], k, 2))
            for copy in self.c3:
                copy.start()
            self.start_y(2)
        if n == 4:
            for s in range(2):
                self.c3[s].wait_recv()
                self.c4[s].start()
        if n == 5:
            for copy in self.c3[2:]:
                copy.wait_recv()
            for k in range(NY):
                yd = here.yplus(k)
                self.put(k, 5, self.three[0, yd])
                self.put(k, 6, self.three[1, yd])
            self.start_y(3)
        if n == 6:
            for copy in self.c4:
                copy.wait_recv()
            for k in range(NY):
                yd = here.yplus(k)
                low = lax.rem(yd, 2)
                self.put(k, 7, jnp.where(yd < 2, self.four[0, low], self.four[1, low]))
            self.start_y(4)
        if n == 7:
            for piece in self.cy:
                for copy in piece:
                    copy.wait_recv()
        if n == 8:
            for copy in self.c1 + self.c2 + self.c3 + self.c4:
                copy.wait_send()
            for piece in self.cy:
                for copy in piece:
                    copy.wait_send()


RETURN_PIECES = ((7, 8), (5, 7), (3, 5), (1, 3), (0, 1))


class Return:
    scratch = ((2, 2), (6, 2), (8, 2), (8, 2), (8, 2), (8, 2))

    def __init__(self, here, copies, table, sent, held, out, bufs):
        self.here, self.table, self.held, self.out = here, table, held, out
        four, three, two, one, out2, out1 = bufs
        self.four, self.three, self.two, self.one = four, three, two, one
        self.out2, self.out1 = out2, out1
        mk = copies.make
        ways = (here.at_z(-1), here.at_z(1))
        h = NB // 2
        self.cy = []
        for a, b in RETURN_PIECES:
            self.cy.append(
                [
                    mk(sent.at[k - 1, pl.ds(a, b - a)], held.at[k, pl.ds(a, b - a)], here.at_y(-k))
                    for k in (2, 1, 3)
                ]
            )
        self.c4, self.c3, self.c2, self.c1 = [], [], [], []
        for s, way in enumerate(ways):
            for i in range(2):
                k = lax.rem(2 * s + i + NY - here.y, NY)
                self.c4.append(mk(held.at[k, 7], four.at[s, i], way))
        for s, way in enumerate(ways):
            self.c3.append(mk(held.at[:, 5 + s], three.at[s, pl.ds(0, 4)], way))
        for s, way in enumerate(ways):
            self.c3.append(mk(four.at[s], three.at[s, pl.ds(4, 2)], way))
        for part in range(2):
            for s, way in enumerate(ways):
                self.c2.append(
                    mk(out2.at[s, pl.ds(part * h, h)], two.at[s, pl.ds(part * h, h)], way)
                )
        for part in range(2):
            for s, way in enumerate(ways):
                self.c1.append(
                    mk(out1.at[s, pl.ds(part * h, h)], one.at[s, pl.ds(part * h, h)], way)
                )

    def start_y(self, piece):
        for copy in self.cy[piece]:
            copy.start()

    def wait_y(self, piece):
        for copy in self.cy[piece]:
            copy.wait_recv()

    @staticmethod
    def total(b, bases, terms):
        acc = None
        for value in bases:
            value = value.astype(jnp.float32)
            acc = value if acc is None else acc + value
        for pick, ref in terms:
            value = ref[...].astype(jnp.float32)
            value = jnp.where(pick == b, value, jnp.zeros_like(value))
            acc = value if acc is None else acc + value
        return acc.astype(jnp.bfloat16)

    def here_terms(self, e, sz):
        return [
            (self.here.pick(self.table, 0, k, sz), self.held.at[k, e]) for k in range(NY)
        ]

    def step(self, n):
        here, table = self.here, self.table
        h = NB // 2
        if n == 1:
            self.wait_y(0)
            for copy in self.c4:
                copy.start()
        if n == 2:
            self.wait_y(1)
            for copy in self.c3[:2]:
                copy.start()
        if n == 3:
            for copy in self.c4:
                copy.wait_recv()
            for copy in self.c3[2:]:
                copy.start()
        if n in (4, 5):
            part = n - 4
            if n == 4:
                self.wait_y(2)
                for copy in self.c3:
                    copy.wait_recv()
            for s, d in ((0, 1), (1, -1)):
                terms = self.here_terms(3 + s, -2 * d)
                for k in range(4):
                    terms.append((here.pick(table, d, k, -2 * d), self.three.at[s, k]))
                for i in range(2):
                    pick = here.pick_abs(table, 2 * d, 2 * s + i, -2 * d)
                    terms.append((pick, self.three.at[s, 4 + i]))
                for b in range(part * h, part * h + h):
                    self.out2[s, b] = self.total(b, [], terms)
            for s in range(2):
                self.c2[part * 2 + s].start()
        if n in (6, 7):
            part = n - 6
            if n == 6:
                self.wait_y(3)
            for s, d in ((0, 1), (1, -1)):
                self.c2[part * 2 + s].wait_recv()
                terms = self.here_terms(1 + s, -d)
                for b in range(part * h, part * h + h):
                    self.out1[s, b] = self.total(b, [self.two[s, b]], terms)
            for s in range(2):
                self.c1[part * 2 + s].start()
        if n in (8, 9):
            part = n - 8
            if n == 8:
                self.wait_y(4)
            for s in range(2):
                self.c1[part * 2 + s].wait_recv()
            terms = self.here_terms(0, 0)
            for b in range(part * h, part * h + h):
                self.out[b] = self.total(b, [self.one[0, b], self.one[1, b]], terms)
        if n == 10:
            for copy in self.c4 + self.c3 + self.c2 + self.c1:
                copy.wait_send()
            for piece in self.cy:
                for copy in piece:
                    copy.wait_send()


def rows_at(i, size):
    return pl.ds(pl.multiple_of(i * size, size), size)


def routes(view, sv_ref, sb_ref, pack_ref):
    slots, views = sv_ref.shape
    sv, sb = sv_ref[...], sb_ref[...]
    wide = (views, views)
    source = lax.broadcasted_iota(jnp.int32, wide, 0)
    table = jnp.full(wide, -1, jnp.int32)
    for j in range(slots):
        same = jnp.broadcast_to(sv[j : j + 1, :], wide) == source
        table = jnp.where(same, jnp.broadcast_to(sb[j : j + 1, :], wide), table)
    pack_ref[0:views, 0:views] = table
    lanes = lax.broadcasted_iota(jnp.int32, sv.shape, 1)
    own = jnp.sum(jnp.where(lanes == view, sv, 0), axis=1, keepdims=True)
    own = jnp.broadcast_to(own, (slots, BLOCK))
    dz = (view // NY - own // NY + NZ) & (NZ - 1)
    dy = ((view & (NY - 1)) - (own & (NY - 1)) + NY) & (NY - 1)
    near = jnp.where(dz == 0, 0, jnp.where(dz <= NZ // 2, 2 * dz - 1, 2 * NZ - 2 * dz))
    place = dy * NZ + near
    turn = (NZ - 1 - near) * NY + dy
    lane = lax.broadcasted_iota(jnp.int32, place.shape, 1)
    taken = jnp.max(jnp.where(turn == lane, 1, 0), axis=0, keepdims=True)
    taken = jnp.broadcast_to(taken, place.shape)
    rank = jnp.sum(jnp.where(lane < turn, taken, 0), axis=1, keepdims=True)
    rank = jnp.broadcast_to(rank, place.shape)
    place_of = jnp.max(jnp.where(rank == lane, place, 0), axis=0, keepdims=True)
    rank_of = jnp.max(jnp.where(place == lane, rank, 0), axis=0, keepdims=True)
    pack_ref[views : views + 8, :] = jnp.broadcast_to(place_of, (8, BLOCK))
    pack_ref[views + 8 : views + 16, :] = jnp.broadcast_to(rank_of, (8, BLOCK))


def layer_kernel(
    sv_ref, sb_ref, q_hbm, k_hbm, v_hbm, w_hbm, og_hbm,
    mixed_hbm, dq_hbm, ok_hbm, ov_hbm,
    *scratch,
):
    fbk, fbv, rbk, rbv = scratch[:6], scratch[6:12], scratch[12:18], scratch[18:24]
    (
        k_own, v_own, og_own, q_s, w_rows, w_cols,
        got_k, got_v, og_all, at_all, sent_k, sent_v, held_k, held_v,
        qm, qtm, dam, datm, k_s, kt_s, v_s, vt_s, s_s, p_s,
        att_t, dq_t, grad_s, att_s, mixed_ref, dq_ref, ok_ref, ov_ref, inv_s, delta_s, pack_v, pack,
        send, recv, local,
    ) = scratch[24:]
    here = Place()
    copies = Copies(send, recv)
    slots, views = sv_ref.shape
    keys = slots * BLOCK
    tokens = q_s.shape[0]
    chunks = keys // KC
    mine = pl.ds(pl.multiple_of(here.head * COLS, COLS), COLS)

    loads = [
        pltpu.make_async_copy(src, dst, local.at[i])
        for i, (src, dst) in enumerate(
            (
                (k_hbm, k_own),
                (og_hbm, og_own),
                (v_hbm, v_own),
                (q_hbm, q_s),
                (w_hbm.at[mine, :], w_rows),
                (w_hbm.at[:, mine], w_cols),
            )
        )
    ]
    for load in loads:
        load.start()
    stores = [
        pltpu.make_async_copy(src, dst, local.at[len(loads) + 1 + i])
        for i, (src, dst) in enumerate(
            (
                (dq_ref, dq_hbm),
                (mixed_ref, mixed_hbm),
                (ov_ref, ov_hbm),
                (ok_ref.at[pl.ds(0, NB // 2)], ok_hbm.at[pl.ds(0, NB // 2)]),
                (ok_ref.at[pl.ds(NB // 2, NB // 2)], ok_hbm.at[pl.ds(NB // 2, NB // 2)]),
            )
        )
    ]
    arrived = greet(here)
    tables = pltpu.make_async_copy(pack_v, pack, local.at[len(loads)])
    routes(here.view, sv_ref, sb_ref, pack_v)
    tables.start()

    og = Gather(here, copies, og_own, og_all)
    fk = Fetch(here, copies, pack, k_own, got_k, fbk)
    fv = Fetch(here, copies, pack, v_own, got_v, fbv)
    at = Gather(here, copies, att_s, at_all)
    rk = Return(here, copies, pack, sent_k, held_k, ok_ref, rbk)
    rv = Return(here, copies, pack, sent_v, held_v, ov_ref, rbv)

    arrived()
    loads[0].wait()
    fk.offer(0)
    fk.offer(1)
    loads[1].wait()
    og.step(0)
    tables.wait()
    fk.step(0)
    loads[2].wait()
    fv.step(0)
    loads[3].wait()
    q = q_s[...]
    lane = lax.broadcasted_iota(jnp.int32, q.shape, 1) // HEAD_DIM
    for h in range(2):
        part = jnp.where(lane == h, q, jnp.zeros_like(q))
        qm[h] = part
        qtm[h] = part.T
    fk.step(1)
    fk.step(2)
    fv.offer(0)
    og.step(1)
    fk.step(3)
    og.step(2)
    loads[4].wait()
    og.step(3)

    def project(i, carry):
        rows = rows_at(i, QB)
        acc = None
        for g in range(2 * NX):
            part = lax.dot_general(
                og_all[g, rows, :],
                w_rows[:, pl.ds(g * COLS, COLS)],
                (((1,), (1,)), ((), ())),
                preferred_element_type=jnp.float32,
            )
            acc = part if acc is None else acc + part
        da = acc.astype(BF)
        half = lax.broadcasted_iota(jnp.int32, da.shape, 1) // HEAD_DIM
        for h in range(2):
            part = jnp.where(half == h, da, jnp.zeros_like(da))
            dam[h, rows, :] = part
            datm[h, :, rows] = part.T
        return carry

    lax.fori_loop(0, tokens // QB, project, 0)
    fk.step(4)
    fv.offer(1)
    fk.step(5)
    fv.step(1)
    fk.step(6)
    fv.step(2)
    fk.step(7)
    for j in range(slots):
        k_s[pl.ds(j * BLOCK, BLOCK), :] = got_k[pack[views, j]]

    tiles = tokens // QB
    turns = SCALE * LOG2E

    def score(h, cols, c, top):
        rows = pl.ds(c * KC, KC)
        s = dot(k_s[rows, :], qtm[h, :, cols])
        s_s[h, rows, :] = s
        return jnp.maximum(top, jnp.max(s, axis=0, keepdims=True))

    lowest = jnp.full((1, QB), -jnp.inf, F32)

    def tile(h, cols, top, other, other_cols):
        shift = top * turns
        total = jnp.zeros((1, QB), F32)
        other_top = lowest
        for c in range(chunks):
            other_top = score(other, other_cols, c, other_top)
            rows = pl.ds(c * KC, KC)
            e = jnp.exp2(s_s[h, rows, :] * turns - shift)
            p_s[h, rows, cols] = e.astype(BF)
            total = total + jnp.sum(e, axis=0, keepdims=True)
        inv = jnp.broadcast_to(1.0 / total, (8, QB))
        inv_s[h, :, cols] = inv
        down = inv.T[:, 0:1]
        dam[h, cols, :] = (dam[h, cols, :].astype(F32) * down).astype(BF)
        qm[h, cols, :] = (qm[h, cols, :].astype(F32) * down).astype(BF)
        return other_top

    def forward(i, top):
        cols = rows_at(i, QB)
        after = rows_at(jnp.minimum(i + 1, tiles - 1), QB)
        top = tile(0, cols, top, 1, cols)

        @pl.when(i == 1)
        def _():
            fv.step(3)

        return tile(1, cols, top, 0, after)

    top = lowest
    for c in range(chunks):
        top = score(0, pl.ds(0, QB), c, top)
    lax.fori_loop(0, tiles, forward, top)

    wide = 4 * BLOCK

    def grads(c, right, scale):
        rows = rows_at(c, wide)
        g = dot(p_s[0, rows, :], right[0]) + dot(p_s[1, rows, :], right[1])
        if scale is not None:
            g = g * scale
        g = g.astype(BF)
        for b in range(4):
            grad_s[c * 4 + b] = g[b * BLOCK : (b + 1) * BLOCK, :]

    def hand_out(sent, held, low, high):
        for e in range(low, high):
            held[0, e] = grad_s[pack[views + 8, e]]
            for k in range(1, NY):
                sent[k - 1, e] = grad_s[pack[views + 8, k * NZ + e]]

    def value_grads(c, carry):
        @pl.when(c == 1)
        def _():
            hand_out(sent_v, held_v, 7, 8)
            rv.start_y(0)

        @pl.when(c == 3)
        def _():
            hand_out(sent_v, held_v, 5, 7)
            rv.start_y(1)

        grads(c, dam, None)
        return carry

    fv.step(4)
    lax.fori_loop(0, keys // wide, value_grads, 0)
    fv.step(5)
    rv.step(1)
    fv.step(6)
    hand_out(sent_v, held_v, 0, 5)
    rv.start_y(2)
    rv.step(2)
    rv.step(3)
    rv.start_y(3)
    rv.start_y(4)
    for j in range(slots):
        kt_s[:, pl.ds(j * BLOCK, BLOCK)] = k_s[pl.ds(j * BLOCK, BLOCK), :].T
    fv.step(7)
    for j in range(slots):
        rows = pl.ds(j * BLOCK, BLOCK)
        block = got_v[pack[views, j]]
        v_s[rows, :] = block
        vt_s[:, rows] = block.T

    def attend(i, carry):
        @pl.when(i == 3)
        def _():
            rv.step(4)

        cols = rows_at(i, QB)
        for h in range(2):
            band = pl.ds(h * HEAD_DIM, HEAD_DIM)
            att = dot(vt_s[band, :], p_s[h, :, cols]) * inv_s[h, 0:1, cols]
            att = att.astype(BF)
            att_t[band, cols] = att
            delta = jnp.sum(
                att.astype(F32) * datm[h, band, cols].astype(F32), axis=0, keepdims=True
            )
            delta_s[h, :, cols] = jnp.broadcast_to(delta, (8, QB))
        return carry

    lax.fori_loop(0, tiles, attend, 0)
    att_s[...] = att_t[...].T
    at.step(0)
    rv.step(5)

    def key_grads(c, carry):
        @pl.when(c == 1)
        def _():
            hand_out(sent_k, held_k, 7, 8)
            rk.start_y(0)

        @pl.when(c == 3)
        def _():
            hand_out(sent_k, held_k, 5, 7)
            rk.start_y(1)
            rk.step(1)
            rv.step(6)

        rows = rows_at(c, wide)
        for h in range(2):
            for i in range(tiles):
                cols = pl.ds(i * QB, QB)
                dp = dot(v_s[rows, :], datm[h, :, cols]) - delta_s[h, 0:1, cols]
                p_s[h, rows, cols] = (p_s[h, rows, cols].astype(F32) * dp).astype(BF)
        grads(c, qm, SCALE)
        return carry

    lax.fori_loop(0, keys // wide, key_grads, 0)
    hand_out(sent_k, held_k, 0, 5)
    rk.start_y(2)
    rk.start_y(3)
    rk.start_y(4)
    at.step(1)

    def query_grads(i, carry):
        @pl.when(i == 3)
        def _():
            rk.step(2)

        cols = rows_at(i, QB)
        for h in range(2):
            band = pl.ds(h * HEAD_DIM, HEAD_DIM)
            dq = dot(kt_s[band, :], p_s[h, :, cols]) * (inv_s[h, 0:1, cols] * SCALE)
            dq_t[band, cols] = dq.astype(BF)
        return carry

    lax.fori_loop(0, tiles, query_grads, 0)
    rk.step(3)
    rv.step(7)
    dq_ref[...] = dq_t[...].T
    stores[0].start()
    at.step(2)
    rk.step(4)
    rk.step(5)
    loads[5].wait()
    at.step(3)

    def mix(i, carry):
        rows = rows_at(i, QB)
        acc = None
        for g in range(2 * NX):
            part = dot(at_all[g, rows, :], w_cols[pl.ds(g * COLS, COLS), :])
            acc = part if acc is None else acc + part
        mixed_ref[rows, :] = acc.astype(BF)
        return carry

    lax.fori_loop(0, tokens // QB, mix, 0)
    stores[1].start()
    rk.step(6)
    rv.step(8)
    rv.step(9)
    stores[2].start()
    rk.step(7)
    fk.step(8)
    fv.step(8)
    og.step(4)
    at.step(4)
    rv.step(10)
    rk.step(8)
    stores[3].start()
    rk.step(9)
    stores[4].start()
    rk.step(10)
    for store in stores:
        store.wait()


def layer(sv, sb, q, k, v, w, og):
    tokens = q.shape[0]
    slots, views = sv.shape
    keys = slots * BLOCK
    hbm = pl.BlockSpec(memory_space=pl.ANY)
    vm = pl.BlockSpec(memory_space=pltpu.VMEM)

    def vmem(*shape, dtype=BF):
        return pltpu.VMEM(shape, dtype)

    def bufs(cls):
        return [vmem(b, a, BLOCK, COLS) for a, b in cls.scratch]

    rows = jax.ShapeDtypeStruct((tokens, COLS), BF)
    cut = jax.ShapeDtypeStruct((NB, BLOCK, COLS), BF)
    return pl.pallas_call(
        layer_kernel,
        out_shape=(rows, rows, cut, cut),
        in_specs=[vm, vm] + [hbm] * 5,
        out_specs=(hbm,) * 4,
        scratch_shapes=bufs(Fetch) + bufs(Fetch) + bufs(Return) + bufs(Return) + [
            vmem(NB, BLOCK, COLS),
            vmem(NB, BLOCK, COLS),
            vmem(tokens, COLS),
            vmem(tokens, COLS),
            vmem(COLS, w.shape[1]),
            vmem(w.shape[0], COLS),
            vmem(NY * NZ, BLOCK, COLS),
            vmem(NY * NZ, BLOCK, COLS),
            vmem(2 * NX, tokens, COLS),
            vmem(2 * NX, tokens, COLS),
            vmem(NY - 1, NZ, BLOCK, COLS),
            vmem(NY - 1, NZ, BLOCK, COLS),
            vmem(NY, NZ, BLOCK, COLS),
            vmem(NY, NZ, BLOCK, COLS),
            vmem(2, tokens, COLS),
            vmem(2, COLS, tokens),
            vmem(2, tokens, COLS),
            vmem(2, COLS, tokens),
            vmem(keys, COLS),
            vmem(COLS, keys),
            vmem(keys, COLS),
            vmem(COLS, keys),
            vmem(2, keys, QB, dtype=F32),
            vmem(2, keys, tokens),
            vmem(COLS, tokens),
            vmem(COLS, tokens),
            vmem(slots, BLOCK, COLS),
            vmem(tokens, COLS),
            vmem(tokens, COLS),
            vmem(tokens, COLS),
            vmem(NB, BLOCK, COLS),
            vmem(NB, BLOCK, COLS),
            vmem(2, 8, tokens, dtype=F32),
            vmem(2, 8, tokens, dtype=F32),
            vmem(views + 16, BLOCK, dtype=jnp.int32),
            pltpu.SMEM((views + 16, BLOCK), jnp.int32),
            pltpu.SemaphoreType.DMA((136,)),
            pltpu.SemaphoreType.DMA((136,)),
            pltpu.SemaphoreType.DMA((12,)),
        ],
        compiler_params=pltpu.CompilerParams(
            collective_id=0, has_side_effects=True, vmem_limit_bytes=56 * 2**20
        ),
        name="layer",
    )(sv, sb, q, k, v, w, og)


def finish_kernel(*refs):
    sems = refs[-1]
    n = (len(refs) - 1) // 2
    moves = [pltpu.make_async_copy(refs[i], refs[n + i], sems.at[i]) for i in range(n)]
    for move in moves:
        move.start()
    for move in moves:
        move.wait()


def finish(*arrays):
    vm = pl.BlockSpec(memory_space=pltpu.VMEM)
    hbm = pl.BlockSpec(memory_space=pl.ANY)
    return pl.pallas_call(
        finish_kernel,
        out_shape=tuple(jax.ShapeDtypeStruct(a.shape, a.dtype) for a in arrays),
        in_specs=[vm] * len(arrays),
        out_specs=(hbm,) * len(arrays),
        scratch_shapes=[pltpu.SemaphoreType.DMA((len(arrays),))],
        name="finish",
    )(*arrays)


def body(query_rows, key_rows, value_rows, out_weight, out_grad, source_view, source_block):
    cut = (NB, BLOCK, COLS)
    mixed, dq, kg, vg = finish(*layer(
        source_view.T, source_block.T,
        query_rows, key_rows.reshape(cut), value_rows.reshape(cut), out_weight, out_grad,
    ))
    return mixed, dq, kg.reshape(query_rows.shape), vg.reshape(query_rows.shape)


def solution(mesh):
    spread = P("view", "head")
    return jax.shard_map(
        body,
        mesh=mesh,
        in_specs=(spread, spread, spread, P(), spread, P(), P()),
        out_specs=(spread, spread, spread, spread),
        check_vma=False,
    )
```

```python
import jax
import jax.numpy as jnp
from jax import lax
from jax.experimental import pallas as pl
from jax.experimental.pallas import tpu as pltpu
from jax.sharding import PartitionSpec as P

HEAD_DIM = 64
BLOCK = 128
COLS = 2 * HEAD_DIM
SCALE = HEAD_DIM ** -0.5
LOG2E = 1.4426950408889634
QB = 256
KC = 256
BF = jnp.bfloat16
F32 = jnp.float32


def dot(a, b):
    return jnp.dot(a, b, preferred_element_type=jnp.float32)


MESH = pl.DeviceIdType.MESH
NZ, NY, NX = 8, 4, 4
NB = 8


class Copies:
    def __init__(self, send, recv, sends, recvs):
        self.send, self.recv = send, recv
        self.sends, self.recvs = list(sends), list(recvs)

    def make(self, src, dst, device):
        return pltpu.make_async_remote_copy(
            src_ref=src,
            dst_ref=dst,
            send_sem=self.send.at[self.sends.pop(0)],
            recv_sem=self.recv.at[self.recvs.pop(0)],
            device_id=device,
            device_id_type=MESH,
        )


class Place:
    def __init__(self):
        view = lax.axis_index("view")
        head = lax.axis_index("head")
        self.view, self.head = view, head
        self.z, self.y = view // NY, lax.rem(view, NY)
        self.x, self.c = head // 2, lax.rem(head, 2)

    def zplus(self, d):
        return lax.rem(self.z + d + NZ, NZ)

    def yplus(self, k):
        return lax.rem(self.y + k + NY, NY)

    def at_z(self, d):
        return {"view": self.zplus(d) * NY + self.y}

    def at_y(self, k):
        return {"view": self.z * NY + self.yplus(k)}

    def at_x(self, d):
        return {"head": lax.rem(self.x + d + NX, NX) * 2 + self.c}

    def partner(self):
        return {"head": self.x * 2 + 1 - self.c}

    def pick(self, table, dz, k, sz):
        taker = self.zplus(dz) * NY + self.yplus(k)
        return table[self.zplus(sz) * NY + self.y, taker]

    def pick_abs(self, table, dz, yd, sz):
        taker = self.zplus(dz) * NY + yd
        return table[self.zplus(sz) * NY + self.y, taker]


def greet(here):
    barrier = pltpu.get_barrier_semaphore()
    peers = [here.at_z(1), here.at_z(-1), here.at_y(1), here.at_y(2), here.at_y(3)]
    peers += [here.at_x(1), here.at_x(-1), here.partner()]
    for peer in peers:
        pl.semaphore_signal(barrier, inc=1, device_id=peer, device_id_type=MESH)
    return lambda: pl.semaphore_wait(barrier, len(peers))


class Gather:
    def __init__(self, here, copies, own, full):
        rows = own.shape[0]
        half = rows // 2
        x, c = here.x, here.c
        me = here.head
        left = lax.rem(x + NX - 1, NX) * 2 + c
        right = lax.rem(x + 1, NX) * 2 + c
        far = lax.rem(x + 2, NX) * 2 + c
        lo, hi = pl.ds(0, half), pl.ds(half, half)
        self.own, self.full, self.me = own, full, me
        mk = copies.make
        self.first = [
            mk(own, full.at[me], here.at_x(1)),
            mk(own, full.at[me], here.at_x(-1)),
        ]
        self.second = [
            mk(full.at[left, lo], full.at[left, lo], here.at_x(1)),
            mk(full.at[right, hi], full.at[right, hi], here.at_x(-1)),
        ]
        self.across = [
            mk(own, full.at[me], here.partner()),
            mk(full.at[left], full.at[left], here.partner()),
            mk(full.at[right], full.at[right], here.partner()),
            mk(full.at[far], full.at[far], here.partner()),
        ]

    def step(self, n):
        if n == 0:
            for copy in self.first:
                copy.start()
            self.across[0].start()
            self.full[self.me] = self.own[...]
        if n == 1:
            for copy in self.first:
                copy.wait_recv()
            for copy in self.second:
                copy.start()
            self.across[1].start()
            self.across[2].start()
        if n == 2:
            for copy in self.second:
                copy.wait_recv()
            self.across[3].start()
        if n == 3:
            for copy in self.across:
                copy.wait_recv()
        if n == 4:
            for copy in self.first + self.second + self.across:
                copy.wait_send()


FETCH_PIECES = ((0, 1), (1, 3), (3, 5), (5, 7), (7, 8))


class Fetch:
    scratch = ((8, 2), (8, 2), (6, 2), (2, 2), (6, 2), (NB, 3))

    def __init__(self, here, copies, table, own, got, bufs):
        self.here, self.table, self.own, self.got = here, table, own, got
        one, two, three, four, fwd, stage = bufs
        self.one, self.two, self.three, self.four = one, two, three, four
        self.fwd, self.stage = fwd, stage
        mk = copies.make
        ways = (here.at_z(1), here.at_z(-1))
        h = NB // 2
        self.c1, self.c2, self.c3, self.c4 = [], [], [], []
        for part in range(2):
            for s, way in enumerate(ways):
                self.c1.append(mk(own.at[pl.ds(part * h, h)], one.at[s, pl.ds(part * h, h)], way))
        for part in range(2):
            for s, way in enumerate(ways):
                self.c2.append(
                    mk(one.at[s, pl.ds(part * h, h)], two.at[s, pl.ds(part * h, h)], way)
                )
        for a, size in ((4, 2), (0, 4)):
            for s, way in enumerate(ways):
                self.c3.append(mk(fwd.at[s, pl.ds(a, size)], three.at[s, pl.ds(a, size)], way))
        for s, way in enumerate(ways):
            self.c4.append(mk(three.at[s, pl.ds(4, 2)], four.at[s], way))
        self.cy = []
        for a, b in FETCH_PIECES:
            self.cy.append(
                [
                    mk(
                        stage.at[k - 1, pl.ds(a, b - a)],
                        got.at[pl.ds(k * NZ + a, b - a)],
                        here.at_y(k),
                    )
                    for k in (2, 1, 3)
                ]
            )

    def put(self, k, e, value):
        if k == 0:
            self.got[e] = value
        else:
            self.stage[k - 1, e] = value

    def select(self, src, k, sz):
        return src[jnp.maximum(self.here.pick(self.table, 0, k, sz), 0)]

    def start_y(self, piece):
        for copy in self.cy[piece]:
            copy.start()

    def offer(self, part):
        for copy in self.c1[part * 2 : part * 2 + 2]:
            copy.start()

    def step(self, n):
        here, table = self.here, self.table
        if n == 0:
            for k in range(NY):
                self.put(k, 0, self.select(self.own, k, 0))
            self.start_y(0)
        if n in (1, 2):
            part = n - 1
            for s in range(2):
                self.c1[part * 2 + s].wait_recv()
                self.c2[part * 2 + s].start()
        if n == 2:
            for k in range(NY):
                self.put(k, 1, self.select(self.one.at[0], k, -1))
                self.put(k, 2, self.select(self.one.at[1], k, 1))
            self.start_y(1)
        if n == 3:
            for copy in self.c2:
                copy.wait_recv()
            for s, d in ((0, 1), (1, -1)):
                src = self.two.at[s]
                for yd in range(4):
                    b = jnp.maximum(here.pick_abs(table, d, yd, -2 * d), 0)
                    self.fwd[s, yd] = src[b]
                for i in range(2):
                    b = jnp.maximum(here.pick_abs(table, 2 * d, 2 * s + i, -2 * d), 0)
                    self.fwd[s, 4 + i] = src[b]
            for k in range(NY):
                self.put(k, 3, self.select(self.two.at[0], k, -2))
                self.put(k, 4, self.select(self.two.at[1], k, 2))
            for copy in self.c3:
                copy.start()
            self.start_y(2)
        if n == 4:
            for s in range(2):
                self.c3[s].wait_recv()
                self.c4[s].start()
        if n == 5:
            for copy in self.c3[2:]:
                copy.wait_recv()
            for k in range(NY):
                yd = here.yplus(k)
                self.put(k, 5, self.three[0, yd])
                self.put(k, 6, self.three[1, yd])
            self.start_y(3)
        if n == 6:
            for copy in self.c4:
                copy.wait_recv()
            for k in range(NY):
                yd = here.yplus(k)
                low = lax.rem(yd, 2)
                self.put(k, 7, jnp.where(yd < 2, self.four[0, low], self.four[1, low]))
            self.start_y(4)
        if n == 7:
            for piece in self.cy:
                for copy in piece:
                    copy.wait_recv()
        if n == 8:
            for copy in self.c1 + self.c2 + self.c3 + self.c4:
                copy.wait_send()
            for piece in self.cy:
                for copy in piece:
                    copy.wait_send()


RETURN_PIECES = ((7, 8), (5, 7), (3, 5), (1, 3), (0, 1))


class Return:
    scratch = ((2, 2), (6, 2), (8, 2), (8, 2), (8, 2), (8, 2))

    def __init__(self, here, copies, table, sent, held, out, bufs):
        self.here, self.table, self.held, self.out = here, table, held, out
        four, three, two, one, out2, out1 = bufs
        self.four, self.three, self.two, self.one = four, three, two, one
        self.out2, self.out1 = out2, out1
        mk = copies.make
        ways = (here.at_z(-1), here.at_z(1))
        h = NB // 2
        self.cy = []
        for a, b in RETURN_PIECES:
            self.cy.append(
                [
                    mk(sent.at[k - 1, pl.ds(a, b - a)], held.at[k, pl.ds(a, b - a)], here.at_y(-k))
                    for k in (2, 1, 3)
                ]
            )
        self.c4, self.c3, self.c2, self.c1 = [], [], [], []
        for s, way in enumerate(ways):
            for i in range(2):
                k = lax.rem(2 * s + i + NY - here.y, NY)
                self.c4.append(mk(held.at[k, 7], four.at[s, i], way))
        for s, way in enumerate(ways):
            self.c3.append(mk(held.at[:, 5 + s], three.at[s, pl.ds(0, 4)], way))
        for s, way in enumerate(ways):
            self.c3.append(mk(four.at[s], three.at[s, pl.ds(4, 2)], way))
        for part in range(2):
            for s, way in enumerate(ways):
                self.c2.append(
                    mk(out2.at[s, pl.ds(part * h, h)], two.at[s, pl.ds(part * h, h)], way)
                )
        for part in range(2):
            for s, way in enumerate(ways):
                self.c1.append(
                    mk(out1.at[s, pl.ds(part * h, h)], one.at[s, pl.ds(part * h, h)], way)
                )

    def start_y(self, piece):
        for copy in self.cy[piece]:
            copy.start()

    def wait_y(self, piece):
        for copy in self.cy[piece]:
            copy.wait_recv()

    @staticmethod
    def total(b, bases, terms):
        acc = None
        for value in bases:
            value = value.astype(jnp.float32)
            acc = value if acc is None else acc + value
        for pick, ref in terms:
            value = ref[...].astype(jnp.float32)
            value = jnp.where(pick == b, value, jnp.zeros_like(value))
            acc = value if acc is None else acc + value
        return acc.astype(jnp.bfloat16)

    def here_terms(self, e, sz):
        return [
            (self.here.pick(self.table, 0, k, sz), self.held.at[k, e]) for k in range(NY)
        ]

    def step(self, n):
        here, table = self.here, self.table
        h = NB // 2
        if n == 1:
            self.wait_y(0)
            for copy in self.c4:
                copy.start()
        if n == 2:
            self.wait_y(1)
            for copy in self.c3[:2]:
                copy.start()
        if n == 3:
            for copy in self.c4:
                copy.wait_recv()
            for copy in self.c3[2:]:
                copy.start()
        if n in (4, 5):
            part = n - 4
            if n == 4:
                self.wait_y(2)
                for copy in self.c3:
                    copy.wait_recv()
            for s, d in ((0, 1), (1, -1)):
                terms = self.here_terms(3 + s, -2 * d)
                for k in range(4):
                    terms.append((here.pick(table, d, k, -2 * d), self.three.at[s, k]))
                for i in range(2):
                    pick = here.pick_abs(table, 2 * d, 2 * s + i, -2 * d)
                    terms.append((pick, self.three.at[s, 4 + i]))
                for b in range(part * h, part * h + h):
                    self.out2[s, b] = self.total(b, [], terms)
            for s in range(2):
                self.c2[part * 2 + s].start()
        if n in (6, 7):
            part = n - 6
            if n == 6:
                self.wait_y(3)
            for s, d in ((0, 1), (1, -1)):
                self.c2[part * 2 + s].wait_recv()
                terms = self.here_terms(1 + s, -d)
                for b in range(part * h, part * h + h):
                    self.out1[s, b] = self.total(b, [self.two[s, b]], terms)
            for s in range(2):
                self.c1[part * 2 + s].start()
        if n in (8, 9):
            part = n - 8
            if n == 8:
                self.wait_y(4)
            for s in range(2):
                self.c1[part * 2 + s].wait_recv()
            terms = self.here_terms(0, 0)
            for b in range(part * h, part * h + h):
                self.out[b] = self.total(b, [self.one[0, b], self.one[1, b]], terms)
        if n == 10:
            for copy in self.c4 + self.c3 + self.c2 + self.c1:
                copy.wait_send()
            for piece in self.cy:
                for copy in piece:
                    copy.wait_send()


def rows_at(i, size):
    return pl.ds(pl.multiple_of(i * size, size), size)


def routes(view, sv_ref, sb_ref, pack_ref):
    slots, views = sv_ref.shape
    sv, sb = sv_ref[...], sb_ref[...]
    wide = (views, views)
    source = lax.broadcasted_iota(jnp.int32, wide, 0)
    table = jnp.full(wide, -1, jnp.int32)
    for j in range(slots):
        same = jnp.broadcast_to(sv[j : j + 1, :], wide) == source
        table = jnp.where(same, jnp.broadcast_to(sb[j : j + 1, :], wide), table)
    pack_ref[0:views, 0:views] = table
    lanes = lax.broadcasted_iota(jnp.int32, sv.shape, 1)
    own = jnp.sum(jnp.where(lanes == view, sv, 0), axis=1, keepdims=True)
    own = jnp.broadcast_to(own, (slots, BLOCK))
    dz = (view // NY - own // NY + NZ) & (NZ - 1)
    dy = ((view & (NY - 1)) - (own & (NY - 1)) + NY) & (NY - 1)
    near = jnp.where(dz == 0, 0, jnp.where(dz <= NZ // 2, 2 * dz - 1, 2 * NZ - 2 * dz))
    place = dy * NZ + near
    turn = (NZ - 1 - near) * NY + dy
    lane = lax.broadcasted_iota(jnp.int32, place.shape, 1)
    taken = jnp.max(jnp.where(turn == lane, 1, 0), axis=0, keepdims=True)
    taken = jnp.broadcast_to(taken, place.shape)
    rank = jnp.sum(jnp.where(lane < turn, taken, 0), axis=1, keepdims=True)
    rank = jnp.broadcast_to(rank, place.shape)
    place_of = jnp.max(jnp.where(rank == lane, place, 0), axis=0, keepdims=True)
    rank_of = jnp.max(jnp.where(place == lane, rank, 0), axis=0, keepdims=True)
    pack_ref[views : views + 8, :] = jnp.broadcast_to(place_of, (8, BLOCK))
    pack_ref[views + 8 : views + 16, :] = jnp.broadcast_to(rank_of, (8, BLOCK))


def layer_kernel(
    sv_ref, sb_ref, q_hbm, k_hbm, v_hbm, w_hbm, og_hbm,
    mixed_hbm, dq_hbm, ok_hbm, ov_hbm,
    *scratch,
):
    fbk, fbv, rbk, rbv = scratch[:6], scratch[6:12], scratch[12:18], scratch[18:24]
    (
        k_own, v_own, og_own, q_s, w_rows, w_cols,
        got_k, got_v, og_all, at_all, sent_k, sent_v, held_k, held_v,
        qm, qtm, dam, datm, k_s, kt_s, v_s, vt_s, s_s, p_s,
        att_t, dq_t, grad_s, att_s, mixed_ref, dq_ref, ok_ref, ov_ref, inv_s, delta_s, pack_v, pack,
        send, recv, local,
    ) = scratch[24:]
    here = Place()
    slots, views = sv_ref.shape
    keys = slots * BLOCK
    tokens = q_s.shape[0]
    chunks = keys // KC
    mine = pl.ds(pl.multiple_of(here.head * COLS, COLS), COLS)

    loads = [
        pltpu.make_async_copy(src, dst, local.at[i])
        for i, (src, dst) in enumerate(
            (
                (k_hbm, k_own),
                (og_hbm, og_own),
                (v_hbm, v_own),
                (q_hbm, q_s),
                (w_hbm.at[mine, :], w_rows),
                (w_hbm.at[:, mine], w_cols),
            )
        )
    ]
    for load in loads:
        load.start()
    stores = [
        pltpu.make_async_copy(src, dst, local.at[len(loads) + 1 + i])
        for i, (src, dst) in enumerate(
            (
                (dq_ref, dq_hbm),
                (mixed_ref, mixed_hbm),
                (ov_ref, ov_hbm),
                (ok_ref.at[pl.ds(0, NB // 2)], ok_hbm.at[pl.ds(0, NB // 2)]),
                (ok_ref.at[pl.ds(NB // 2, NB // 2)], ok_hbm.at[pl.ds(NB // 2, NB // 2)]),
            )
        )
    ]
    arrived = greet(here)
    tables = pltpu.make_async_copy(pack_v, pack, local.at[len(loads)])
    routes(here.view, sv_ref, sb_ref, pack_v)
    tables.start()

    def span(a, n):
        return list(range(a, a + n))

    gat = span(58, 8)
    og = Gather(here, Copies(send, recv, span(62, 8), gat), og_own, og_all)
    at = Gather(here, Copies(send, recv, span(62, 8), span(66, 8)), att_s, at_all)
    fk = Fetch(here, Copies(send, recv, span(0, 29), span(0, 29)), pack, k_own, got_k, fbk)
    fv = Fetch(here, Copies(send, recv, span(31, 29), span(29, 29)), pack, v_own, got_v, fbv)
    rv = Return(
        here,
        Copies(send, recv, span(0, 31), span(0, 14) + gat[0:1] + span(14, 15) + gat[1:2]),
        pack, sent_v, held_v, ov_ref, rbv,
    )
    rk = Return(
        here,
        Copies(send, recv, span(31, 31), span(29, 14) + gat[2:3] + span(43, 15) + gat[3:4]),
        pack, sent_k, held_k, ok_ref, rbk,
    )

    arrived()
    loads[0].wait()
    fk.offer(0)
    fk.offer(1)
    loads[1].wait()
    og.step(0)
    tables.wait()
    fk.step(0)
    loads[2].wait()
    fv.step(0)
    loads[3].wait()
    q = q_s[...]
    lane = lax.broadcasted_iota(jnp.int32, q.shape, 1) // HEAD_DIM
    for h in range(2):
        part = jnp.where(lane == h, q, jnp.zeros_like(q))
        qm[h] = part
        qtm[h] = part.T
    fk.step(1)
    fk.step(2)
    fv.offer(0)
    og.step(1)
    fk.step(3)
    og.step(2)
    loads[4].wait()
    og.step(3)

    def project(i, carry):
        rows = rows_at(i, QB)
        acc = None
        for g in range(2 * NX):
            part = lax.dot_general(
                og_all[g, rows, :],
                w_rows[:, pl.ds(g * COLS, COLS)],
                (((1,), (1,)), ((), ())),
                preferred_element_type=jnp.float32,
            )
            acc = part if acc is None else acc + part
        da = acc.astype(BF)
        half = lax.broadcasted_iota(jnp.int32, da.shape, 1) // HEAD_DIM
        for h in range(2):
            part = jnp.where(half == h, da, jnp.zeros_like(da))
            dam[h, rows, :] = part
            datm[h, :, rows] = part.T
        return carry

    lax.fori_loop(0, tokens // QB, project, 0)
    fk.step(4)
    fv.offer(1)
    fk.step(5)
    fv.step(1)
    fk.step(6)
    fv.step(2)
    fk.step(7)
    for j in range(slots):
        k_s[pl.ds(j * BLOCK, BLOCK), :] = got_k[pack[views, j]]

    tiles = tokens // QB
    turns = SCALE * LOG2E

    def score(h, cols, c, top):
        rows = pl.ds(c * KC, KC)
        s = dot(k_s[rows, :], qtm[h, :, cols])
        s_s[h, rows, :] = s
        return jnp.maximum(top, jnp.max(s, axis=0, keepdims=True))

    lowest = jnp.full((1, QB), -jnp.inf, F32)

    def tile(h, cols, top, other, other_cols):
        shift = top * turns
        total = jnp.zeros((1, QB), F32)
        other_top = lowest
        for c in range(chunks):
            other_top = score(other, other_cols, c, other_top)
            rows = pl.ds(c * KC, KC)
            e = jnp.exp2(s_s[h, rows, :] * turns - shift)
            p_s[h, rows, cols] = e.astype(BF)
            total = total + jnp.sum(e, axis=0, keepdims=True)
        inv = jnp.broadcast_to(1.0 / total, (8, QB))
        inv_s[h, :, cols] = inv
        down = inv.T[:, 0:1]
        dam[h, cols, :] = (dam[h, cols, :].astype(F32) * down).astype(BF)
        qm[h, cols, :] = (qm[h, cols, :].astype(F32) * down).astype(BF)
        return other_top

    def forward(i, top):
        cols = rows_at(i, QB)
        after = rows_at(jnp.minimum(i + 1, tiles - 1), QB)
        top = tile(0, cols, top, 1, cols)

        @pl.when(i == 1)
        def _():
            fv.step(3)

        return tile(1, cols, top, 0, after)

    top = lowest
    for c in range(chunks):
        top = score(0, pl.ds(0, QB), c, top)
    lax.fori_loop(0, tiles, forward, top)

    wide = 4 * BLOCK

    def grads(c, right):
        rows = rows_at(c, wide)
        g = dot(p_s[0, rows, :], right[0]) + dot(p_s[1, rows, :], right[1])
        g = g.astype(BF)
        for b in range(4):
            grad_s[c * 4 + b] = g[b * BLOCK : (b + 1) * BLOCK, :]

    def hand_out(sent, held, low, high):
        for e in range(low, high):
            held[0, e] = grad_s[pack[views + 8, e]]
            for k in range(1, NY):
                sent[k - 1, e] = grad_s[pack[views + 8, k * NZ + e]]

    def value_grads(c, carry):
        @pl.when(c == 1)
        def _():
            hand_out(sent_v, held_v, 7, 8)
            rv.start_y(0)

        @pl.when(c == 3)
        def _():
            hand_out(sent_v, held_v, 5, 7)
            rv.start_y(1)

        grads(c, dam)
        return carry

    fv.step(4)
    fk.step(8)
    og.step(4)
    lax.fori_loop(0, keys // wide, value_grads, 0)
    fv.step(5)
    rv.step(1)
    fv.step(6)
    hand_out(sent_v, held_v, 0, 5)
    rv.start_y(2)
    rv.step(2)
    rv.step(3)
    rv.start_y(3)
    rv.start_y(4)
    for j in range(slots):
        kt_s[:, pl.ds(j * BLOCK, BLOCK)] = k_s[pl.ds(j * BLOCK, BLOCK), :].T
    fv.step(7)
    for j in range(slots):
        rows = pl.ds(j * BLOCK, BLOCK)
        block = got_v[pack[views, j]]
        v_s[rows, :] = block
        vt_s[:, rows] = block.T

    def attend(i, carry):
        @pl.when(i == 3)
        def _():
            rv.step(4)

        cols = rows_at(i, QB)
        for h in range(2):
            band = pl.ds(h * HEAD_DIM, HEAD_DIM)
            att = dot(vt_s[band, :], p_s[h, :, cols]) * inv_s[h, 0:1, cols]
            att = att.astype(BF)
            att_t[band, cols] = att
            delta = jnp.sum(
                att.astype(F32) * datm[h, band, cols].astype(F32), axis=0, keepdims=True
            )
            delta_s[h, :, cols] = jnp.broadcast_to(delta, (8, QB))
        return carry

    lax.fori_loop(0, tiles, attend, 0)
    fv.step(8)
    att_s[...] = att_t[...].T
    at.step(0)
    rv.step(5)

    def key_grads(c, carry):
        @pl.when(c == 1)
        def _():
            hand_out(sent_k, held_k, 7, 8)
            rk.start_y(0)

        @pl.when(c == 3)
        def _():
            hand_out(sent_k, held_k, 5, 7)
            rk.start_y(1)
            rv.step(6)
            rk.step(1)

        rows = rows_at(c, wide)
        total, held = None, None
        for h in range(2):
            for i in range(tiles):
                cols = pl.ds(i * QB, QB)
                dp = dot(v_s[rows, :], datm[h, :, cols])
                if held is not None:
                    part = dot(*held)
                    total = part if total is None else total + part
                dp = dp - delta_s[h, 0:1, cols]
                ds = (p_s[h, rows, cols].astype(F32) * dp).astype(BF)
                p_s[h, rows, cols] = ds
                held = (ds, qm[h, cols, :])
        total = ((total + dot(*held)) * SCALE).astype(BF)
        for b in range(4):
            grad_s[c * 4 + b] = total[b * BLOCK : (b + 1) * BLOCK, :]
        return carry

    lax.fori_loop(0, keys // wide, key_grads, 0)
    hand_out(sent_k, held_k, 0, 5)
    rk.start_y(2)
    rk.start_y(3)
    rk.start_y(4)
    at.step(1)

    def query_grads(i, carry):
        @pl.when(i == 3)
        def _():
            rk.step(2)

        cols = rows_at(i, QB)
        for h in range(2):
            band = pl.ds(h * HEAD_DIM, HEAD_DIM)
            dq = dot(kt_s[band, :], p_s[h, :, cols]) * (inv_s[h, 0:1, cols] * SCALE)
            dq_t[band, cols] = dq.astype(BF)
        return carry

    lax.fori_loop(0, tiles, query_grads, 0)
    rk.step(3)
    rv.step(7)
    dq_ref[...] = dq_t[...].T
    stores[0].start()
    at.step(2)
    rk.step(4)
    rk.step(5)
    loads[5].wait()
    at.step(3)

    def mix(i, carry):
        rows = rows_at(i, QB)
        acc = None
        for g in range(2 * NX):
            part = dot(at_all[g, rows, :], w_cols[pl.ds(g * COLS, COLS), :])
            acc = part if acc is None else acc + part
        mixed_ref[rows, :] = acc.astype(BF)
        return carry

    lax.fori_loop(0, tokens // QB, mix, 0)
    stores[1].start()
    rk.step(6)
    rv.step(8)
    rv.step(9)
    stores[2].start()
    rk.step(7)
    at.step(4)
    rv.step(10)
    rk.step(8)
    stores[3].start()
    rk.step(9)
    stores[4].start()
    rk.step(10)
    for store in stores:
        store.wait()


def layer(sv, sb, q, k, v, w, og):
    tokens = q.shape[0]
    slots, views = sv.shape
    keys = slots * BLOCK
    hbm = pl.BlockSpec(memory_space=pl.ANY)
    vm = pl.BlockSpec(memory_space=pltpu.VMEM)

    def vmem(*shape, dtype=BF):
        return pltpu.VMEM(shape, dtype)

    def bufs(cls):
        return [vmem(b, a, BLOCK, COLS) for a, b in cls.scratch]

    rows = jax.ShapeDtypeStruct((tokens, COLS), BF)
    cut = jax.ShapeDtypeStruct((NB, BLOCK, COLS), BF)
    return pl.pallas_call(
        layer_kernel,
        out_shape=(rows, rows, cut, cut),
        in_specs=[vm, vm] + [hbm] * 5,
        out_specs=(hbm,) * 4,
        scratch_shapes=bufs(Fetch) + bufs(Fetch) + bufs(Return) + bufs(Return) + [
            vmem(NB, BLOCK, COLS),
            vmem(NB, BLOCK, COLS),
            vmem(tokens, COLS),
            vmem(tokens, COLS),
            vmem(COLS, w.shape[1]),
            vmem(w.shape[0], COLS),
            vmem(NY * NZ, BLOCK, COLS),
            vmem(NY * NZ, BLOCK, COLS),
            vmem(2 * NX, tokens, COLS),
            vmem(2 * NX, tokens, COLS),
            vmem(NY - 1, NZ, BLOCK, COLS),
            vmem(NY - 1, NZ, BLOCK, COLS),
            vmem(NY, NZ, BLOCK, COLS),
            vmem(NY, NZ, BLOCK, COLS),
            vmem(2, tokens, COLS),
            vmem(2, COLS, tokens),
            vmem(2, tokens, COLS),
            vmem(2, COLS, tokens),
            vmem(keys, COLS),
            vmem(COLS, keys),
            vmem(keys, COLS),
            vmem(COLS, keys),
            vmem(2, keys, QB, dtype=F32),
            vmem(2, keys, tokens),
            vmem(COLS, tokens),
            vmem(COLS, tokens),
            vmem(slots, BLOCK, COLS),
            vmem(tokens, COLS),
            vmem(tokens, COLS),
            vmem(tokens, COLS),
            vmem(NB, BLOCK, COLS),
            vmem(NB, BLOCK, COLS),
            vmem(2, 8, tokens, dtype=F32),
            vmem(2, 8, tokens, dtype=F32),
            vmem(views + 16, BLOCK, dtype=jnp.int32),
            pltpu.SMEM((views + 16, BLOCK), jnp.int32),
            pltpu.SemaphoreType.DMA((70,)),
            pltpu.SemaphoreType.DMA((74,)),
            pltpu.SemaphoreType.DMA((12,)),
        ],
        compiler_params=pltpu.CompilerParams(
            collective_id=0, has_side_effects=True, vmem_limit_bytes=56 * 2**20
        ),
        name="layer",
    )(sv, sb, q, k, v, w, og)


def finish_kernel(*refs):
    sems = refs[-1]
    n = (len(refs) - 1) // 2
    moves = [pltpu.make_async_copy(refs[i], refs[n + i], sems.at[i]) for i in range(n)]
    for move in moves:
        move.start()
    for move in moves:
        move.wait()


def finish(*arrays):
    vm = pl.BlockSpec(memory_space=pltpu.VMEM)
    hbm = pl.BlockSpec(memory_space=pl.ANY)
    return pl.pallas_call(
        finish_kernel,
        out_shape=tuple(jax.ShapeDtypeStruct(a.shape, a.dtype) for a in arrays),
        in_specs=[vm] * len(arrays),
        out_specs=(hbm,) * len(arrays),
        scratch_shapes=[pltpu.SemaphoreType.DMA((len(arrays),))],
        name="finish",
    )(*arrays)


def body(query_rows, key_rows, value_rows, out_weight, out_grad, source_view, source_block):
    cut = (NB, BLOCK, COLS)
    mixed, dq, kg, vg = finish(*layer(
        source_view.T, source_block.T,
        query_rows, key_rows.reshape(cut), value_rows.reshape(cut), out_weight, out_grad,
    ))
    return mixed, dq, kg.reshape(query_rows.shape), vg.reshape(query_rows.shape)


def solution(mesh):
    spread = P("view", "head")
    return jax.shard_map(
        body,
        mesh=mesh,
        in_specs=(spread, spread, spread, P(), spread, P(), P()),
        out_specs=(spread, spread, spread, spread),
        check_vma=False,
    )
```

```python
import jax
import jax.numpy as jnp
from jax import lax
from jax.experimental import pallas as pl
from jax.experimental.pallas import tpu as pltpu
from jax.sharding import PartitionSpec as P

HEAD_DIM = 64
BLOCK = 128
COLS = 2 * HEAD_DIM
SCALE = HEAD_DIM ** -0.5
LOG2E = 1.4426950408889634
QB = 256
KC = 256
BF = jnp.bfloat16
F32 = jnp.float32


def dot(a, b):
    return jnp.dot(a, b, preferred_element_type=jnp.float32)


MESH = pl.DeviceIdType.MESH
NZ, NY, NX = 8, 4, 4
NB = 8


class Copies:
    def __init__(self, send, recv, sends, recvs):
        self.send, self.recv = send, recv
        self.sends, self.recvs = list(sends), list(recvs)

    def make(self, src, dst, device):
        return pltpu.make_async_remote_copy(
            src_ref=src,
            dst_ref=dst,
            send_sem=self.send.at[self.sends.pop(0)],
            recv_sem=self.recv.at[self.recvs.pop(0)],
            device_id=device,
            device_id_type=MESH,
        )


class Place:
    def __init__(self):
        view = lax.axis_index("view")
        head = lax.axis_index("head")
        self.view, self.head = view, head
        self.z, self.y = view // NY, lax.rem(view, NY)
        self.x, self.c = head // 2, lax.rem(head, 2)

    def zplus(self, d):
        return lax.rem(self.z + d + NZ, NZ)

    def yplus(self, k):
        return lax.rem(self.y + k + NY, NY)

    def at_z(self, d):
        return {"view": self.zplus(d) * NY + self.y}

    def at_y(self, k):
        return {"view": self.z * NY + self.yplus(k)}

    def at_x(self, d):
        return {"head": lax.rem(self.x + d + NX, NX) * 2 + self.c}

    def partner(self):
        return {"head": self.x * 2 + 1 - self.c}

    def pick(self, table, dz, k, sz):
        taker = self.zplus(dz) * NY + self.yplus(k)
        return table[self.zplus(sz) * NY + self.y, taker]

    def pick_abs(self, table, dz, yd, sz):
        taker = self.zplus(dz) * NY + yd
        return table[self.zplus(sz) * NY + self.y, taker]


def greet(here):
    barrier = pltpu.get_barrier_semaphore()
    peers = [here.at_z(1), here.at_z(-1), here.at_y(1), here.at_y(2), here.at_y(3)]
    peers += [here.at_x(1), here.at_x(-1), here.partner()]
    for peer in peers:
        pl.semaphore_signal(barrier, inc=1, device_id=peer, device_id_type=MESH)
    return lambda: pl.semaphore_wait(barrier, len(peers))


class Gather:
    def __init__(self, here, copies, own, full):
        rows = own.shape[0]
        half = rows // 2
        x, c = here.x, here.c
        me = here.head
        left = lax.rem(x + NX - 1, NX) * 2 + c
        right = lax.rem(x + 1, NX) * 2 + c
        far = lax.rem(x + 2, NX) * 2 + c
        lo, hi = pl.ds(0, half), pl.ds(half, half)
        self.own, self.full, self.me = own, full, me
        mk = copies.make
        self.first = [
            mk(own, full.at[me], here.at_x(1)),
            mk(own, full.at[me], here.at_x(-1)),
        ]
        self.second = [
            mk(full.at[left, lo], full.at[left, lo], here.at_x(1)),
            mk(full.at[right, hi], full.at[right, hi], here.at_x(-1)),
        ]
        self.across = [
            mk(own, full.at[me], here.partner()),
            mk(full.at[left], full.at[left], here.partner()),
            mk(full.at[right], full.at[right], here.partner()),
            mk(full.at[far], full.at[far], here.partner()),
        ]

    def step(self, n):
        if n == 0:
            for copy in self.first:
                copy.start()
            self.across[0].start()
            self.full[self.me] = self.own[...]
        if n == 1:
            for copy in self.first:
                copy.wait_recv()
            for copy in self.second:
                copy.start()
            self.across[1].start()
            self.across[2].start()
        if n == 2:
            for copy in self.second:
                copy.wait_recv()
            self.across[3].start()
        if n == 3:
            for copy in self.across:
                copy.wait_recv()
        if n == 4:
            for copy in self.first + self.second + self.across:
                copy.wait_send()


FETCH_PIECES = ((0, 1), (1, 3), (3, 5), (5, 7), (7, 8))


class Fetch:
    scratch = ((8, 2), (8, 2), (6, 2), (2, 2), (6, 2), (NB, 3))

    def __init__(self, here, copies, table, own, got, bufs):
        self.here, self.table, self.own, self.got = here, table, own, got
        one, two, three, four, fwd, stage = bufs
        self.one, self.two, self.three, self.four = one, two, three, four
        self.fwd, self.stage = fwd, stage
        mk = copies.make
        ways = (here.at_z(1), here.at_z(-1))
        h = NB // 2
        self.c1, self.c2, self.c3, self.c4 = [], [], [], []
        for part in range(2):
            for s, way in enumerate(ways):
                self.c1.append(mk(own.at[pl.ds(part * h, h)], one.at[s, pl.ds(part * h, h)], way))
        for part in range(2):
            for s, way in enumerate(ways):
                self.c2.append(
                    mk(one.at[s, pl.ds(part * h, h)], two.at[s, pl.ds(part * h, h)], way)
                )
        for a, size in ((4, 2), (0, 4)):
            for s, way in enumerate(ways):
                self.c3.append(mk(fwd.at[s, pl.ds(a, size)], three.at[s, pl.ds(a, size)], way))
        for s, way in enumerate(ways):
            self.c4.append(mk(three.at[s, pl.ds(4, 2)], four.at[s], way))
        self.cy = []
        for a, b in FETCH_PIECES:
            self.cy.append(
                [
                    mk(
                        stage.at[k - 1, pl.ds(a, b - a)],
                        got.at[pl.ds(k * NZ + a, b - a)],
                        here.at_y(k),
                    )
                    for k in (2, 1, 3)
                ]
            )

    def put(self, k, e, value):
        if k == 0:
            self.got[e] = value
        else:
            self.stage[k - 1, e] = value

    def select(self, src, k, sz):
        return src[jnp.maximum(self.here.pick(self.table, 0, k, sz), 0)]

    def start_y(self, piece):
        for copy in self.cy[piece]:
            copy.start()

    def offer(self, part):
        for copy in self.c1[part * 2 : part * 2 + 2]:
            copy.start()

    def step(self, n):
        here, table = self.here, self.table
        if n == 0:
            for k in range(NY):
                self.put(k, 0, self.select(self.own, k, 0))
            self.start_y(0)
        if n in (1, 2):
            part = n - 1
            for s in range(2):
                self.c1[part * 2 + s].wait_recv()
                self.c2[part * 2 + s].start()
        if n == 2:
            for k in range(NY):
                self.put(k, 1, self.select(self.one.at[0], k, -1))
                self.put(k, 2, self.select(self.one.at[1], k, 1))
            self.start_y(1)
        if n == 3:
            for copy in self.c2:
                copy.wait_recv()
            for s, d in ((0, 1), (1, -1)):
                src = self.two.at[s]
                for yd in range(4):
                    b = jnp.maximum(here.pick_abs(table, d, yd, -2 * d), 0)
                    self.fwd[s, yd] = src[b]
                for i in range(2):
                    b = jnp.maximum(here.pick_abs(table, 2 * d, 2 * s + i, -2 * d), 0)
                    self.fwd[s, 4 + i] = src[b]
            for k in range(NY):
                self.put(k, 3, self.select(self.two.at[0], k, -2))
                self.put(k, 4, self.select(self.two.at[1], k, 2))
            for copy in self.c3:
                copy.start()
            self.start_y(2)
        if n == 4:
            for s in range(2):
                self.c3[s].wait_recv()
                self.c4[s].start()
        if n == 5:
            for copy in self.c3[2:]:
                copy.wait_recv()
            for k in range(NY):
                yd = here.yplus(k)
                self.put(k, 5, self.three[0, yd])
                self.put(k, 6, self.three[1, yd])
            self.start_y(3)
        if n == 6:
            for copy in self.c4:
                copy.wait_recv()
            for k in range(NY):
                yd = here.yplus(k)
                low = lax.rem(yd, 2)
                self.put(k, 7, jnp.where(yd < 2, self.four[0, low], self.four[1, low]))
            self.start_y(4)
        if n == 7:
            for piece in self.cy:
                for copy in piece:
                    copy.wait_recv()
        if n == 8:
            for copy in self.c1 + self.c2 + self.c3 + self.c4:
                copy.wait_send()
            for piece in self.cy:
                for copy in piece:
                    copy.wait_send()


RETURN_PIECES = ((7, 8), (5, 7), (3, 5), (1, 3), (0, 1))


class Return:
    scratch = ((2, 2), (6, 2), (8, 2), (8, 2), (8, 2), (8, 2))

    def __init__(self, here, copies, table, sent, held, out, bufs):
        self.here, self.table, self.held, self.out = here, table, held, out
        four, three, two, one, out2, out1 = bufs
        self.four, self.three, self.two, self.one = four, three, two, one
        self.out2, self.out1 = out2, out1
        mk = copies.make
        ways = (here.at_z(-1), here.at_z(1))
        h = NB // 2
        self.cy = []
        for a, b in RETURN_PIECES:
            self.cy.append(
                [
                    mk(sent.at[k - 1, pl.ds(a, b - a)], held.at[k, pl.ds(a, b - a)], here.at_y(-k))
                    for k in (2, 1, 3)
                ]
            )
        self.c4, self.c3, self.c2, self.c1 = [], [], [], []
        for s, way in enumerate(ways):
            for i in range(2):
                k = lax.rem(2 * s + i + NY - here.y, NY)
                self.c4.append(mk(held.at[k, 7], four.at[s, i], way))
        for k, size in ((0, 1), (1, 3)):
            for s, way in enumerate(ways):
                self.c3.append(
                    mk(held.at[pl.ds(k, size), 5 + s], three.at[s, pl.ds(k, size)], way)
                )
        for s, way in enumerate(ways):
            self.c3.append(mk(four.at[s], three.at[s, pl.ds(4, 2)], way))
        for part in range(2):
            for s, way in enumerate(ways):
                self.c2.append(
                    mk(out2.at[s, pl.ds(part * h, h)], two.at[s, pl.ds(part * h, h)], way)
                )
        for part in range(2):
            for s, way in enumerate(ways):
                self.c1.append(
                    mk(out1.at[s, pl.ds(part * h, h)], one.at[s, pl.ds(part * h, h)], way)
                )

    def start_y(self, piece):
        for copy in self.cy[piece]:
            copy.start()

    def wait_y(self, piece):
        for copy in self.cy[piece]:
            copy.wait_recv()

    @staticmethod
    def total(b, bases, terms):
        acc = None
        for value in bases:
            value = value.astype(jnp.float32)
            acc = value if acc is None else acc + value
        for pick, ref in terms:
            value = ref[...].astype(jnp.float32)
            value = jnp.where(pick == b, value, jnp.zeros_like(value))
            acc = value if acc is None else acc + value
        return acc.astype(jnp.bfloat16)

    def here_terms(self, e, sz):
        return [
            (self.here.pick(self.table, 0, k, sz), self.held.at[k, e]) for k in range(NY)
        ]

    def step(self, n):
        here, table = self.here, self.table
        h = NB // 2
        if n == 0:
            for copy in self.c3[:2]:
                copy.start()
        if n == 1:
            self.wait_y(0)
            for copy in self.c4:
                copy.start()
        if n == 2:
            self.wait_y(1)
            for copy in self.c3[2:4]:
                copy.start()
        if n == 3:
            for copy in self.c4:
                copy.wait_recv()
            for copy in self.c3[4:]:
                copy.start()
        if n in (4, 5):
            part = n - 4
            if n == 4:
                self.wait_y(2)
                for copy in self.c3:
                    copy.wait_recv()
            for s, d in ((0, 1), (1, -1)):
                terms = self.here_terms(3 + s, -2 * d)
                for k in range(4):
                    terms.append((here.pick(table, d, k, -2 * d), self.three.at[s, k]))
                for i in range(2):
                    pick = here.pick_abs(table, 2 * d, 2 * s + i, -2 * d)
                    terms.append((pick, self.three.at[s, 4 + i]))
                for b in range(part * h, part * h + h):
                    self.out2[s, b] = self.total(b, [], terms)
            for s in range(2):
                self.c2[part * 2 + s].start()
        if n in (6, 7):
            part = n - 6
            if n == 6:
                self.wait_y(3)
            for s, d in ((0, 1), (1, -1)):
                self.c2[part * 2 + s].wait_recv()
                terms = self.here_terms(1 + s, -d)
                for b in range(part * h, part * h + h):
                    self.out1[s, b] = self.total(b, [self.two[s, b]], terms)
            for s in range(2):
                self.c1[part * 2 + s].start()
        if n in (8, 9):
            part = n - 8
            if n == 8:
                self.wait_y(4)
            for s in range(2):
                self.c1[part * 2 + s].wait_recv()
            terms = self.here_terms(0, 0)
            for b in range(part * h, part * h + h):
                self.out[b] = self.total(b, [self.one[0, b], self.one[1, b]], terms)
        if n == 10:
            for copy in self.c4 + self.c3 + self.c2 + self.c1:
                copy.wait_send()
            for piece in self.cy:
                for copy in piece:
                    copy.wait_send()


def rows_at(i, size):
    return pl.ds(pl.multiple_of(i * size, size), size)


def routes(view, sv_ref, sb_ref, pack_ref):
    slots, views = sv_ref.shape
    sv, sb = sv_ref[...], sb_ref[...]
    wide = (views, views)
    source = lax.broadcasted_iota(jnp.int32, wide, 0)
    table = jnp.full(wide, -1, jnp.int32)
    for j in range(slots):
        same = jnp.broadcast_to(sv[j : j + 1, :], wide) == source
        table = jnp.where(same, jnp.broadcast_to(sb[j : j + 1, :], wide), table)
    pack_ref[0:views, 0:views] = table
    lanes = lax.broadcasted_iota(jnp.int32, sv.shape, 1)
    own = jnp.sum(jnp.where(lanes == view, sv, 0), axis=1, keepdims=True)
    own = jnp.broadcast_to(own, (slots, BLOCK))
    dz = (view // NY - own // NY + NZ) & (NZ - 1)
    dy = ((view & (NY - 1)) - (own & (NY - 1)) + NY) & (NY - 1)
    near = jnp.where(dz == 0, 0, jnp.where(dz <= NZ // 2, 2 * dz - 1, 2 * NZ - 2 * dz))
    place = dy * NZ + near
    turn = (NZ - 1 - near) * NY + dy
    lane = lax.broadcasted_iota(jnp.int32, place.shape, 1)
    taken = jnp.max(jnp.where(turn == lane, 1, 0), axis=0, keepdims=True)
    taken = jnp.broadcast_to(taken, place.shape)
    rank = jnp.sum(jnp.where(lane < turn, taken, 0), axis=1, keepdims=True)
    rank = jnp.broadcast_to(rank, place.shape)
    place_of = jnp.max(jnp.where(rank == lane, place, 0), axis=0, keepdims=True)
    rank_of = jnp.max(jnp.where(place == lane, rank, 0), axis=0, keepdims=True)
    pack_ref[views : views + 8, :] = jnp.broadcast_to(place_of, (8, BLOCK))
    pack_ref[views + 8 : views + 16, :] = jnp.broadcast_to(rank_of, (8, BLOCK))


def layer_kernel(
    sv_ref, sb_ref, q_hbm, k_hbm, v_hbm, w_hbm, og_hbm,
    mixed_hbm, dq_hbm, ok_hbm, ov_hbm,
    *scratch,
):
    fbk, fbv, rbk, rbv = scratch[:6], scratch[6:12], scratch[12:18], scratch[18:24]
    (
        k_own, v_own, og_own, q_s, w_rows, w_cols,
        got_k, got_v, og_all, at_all, sent_k, sent_v, held_k, held_v,
        qm, qtm, dam, datm, k_s, kt_s, v_s, vt_s, s_s, p_s,
        att_t, dq_t, grad_s, att_s, mixed_ref, dq_ref, ok_ref, ov_ref, inv_s, delta_s, pack_v, pack,
        send, recv, local,
    ) = scratch[24:]
    here = Place()
    slots, views = sv_ref.shape
    keys = slots * BLOCK
    tokens = q_s.shape[0]
    chunks = keys // KC
    mine = pl.ds(pl.multiple_of(here.head * COLS, COLS), COLS)

    loads = [
        pltpu.make_async_copy(src, dst, local.at[i])
        for i, (src, dst) in enumerate(
            (
                (k_hbm, k_own),
                (og_hbm, og_own),
                (v_hbm, v_own),
                (q_hbm, q_s),
                (w_hbm.at[mine, :], w_rows),
                (w_hbm.at[:, mine], w_cols),
            )
        )
    ]
    for load in loads:
        load.start()
    stores = [
        pltpu.make_async_copy(src, dst, local.at[len(loads) + 1 + i])
        for i, (src, dst) in enumerate(
            (
                (dq_ref, dq_hbm),
                (mixed_ref, mixed_hbm),
                (ov_ref, ov_hbm),
                (ok_ref.at[pl.ds(0, NB // 2)], ok_hbm.at[pl.ds(0, NB // 2)]),
                (ok_ref.at[pl.ds(NB // 2, NB // 2)], ok_hbm.at[pl.ds(NB // 2, NB // 2)]),
            )
        )
    ]
    arrived = greet(here)
    tables = pltpu.make_async_copy(pack_v, pack, local.at[len(loads)])
    routes(here.view, sv_ref, sb_ref, pack_v)
    tables.start()

    def span(a, n):
        return list(range(a, a + n))

    gat = span(58, 8)
    og = Gather(here, Copies(send, recv, span(66, 8), gat), og_own, og_all)
    at = Gather(here, Copies(send, recv, span(66, 8), span(66, 8)), att_s, at_all)
    fk = Fetch(here, Copies(send, recv, span(0, 29), span(0, 29)), pack, k_own, got_k, fbk)
    fv = Fetch(here, Copies(send, recv, span(33, 29), span(29, 29)), pack, v_own, got_v, fbv)
    rv = Return(
        here,
        Copies(send, recv, span(0, 33), span(0, 14) + gat[0:1] + span(14, 15) + gat[1:4]),
        pack, sent_v, held_v, ov_ref, rbv,
    )
    rk = Return(
        here,
        Copies(send, recv, span(33, 33), span(29, 14) + gat[4:5] + span(43, 15) + gat[5:8]),
        pack, sent_k, held_k, ok_ref, rbk,
    )

    arrived()
    loads[0].wait()
    fk.offer(0)
    fk.offer(1)
    loads[1].wait()
    og.step(0)
    tables.wait()
    fk.step(0)
    loads[2].wait()
    fv.step(0)
    loads[3].wait()
    q = q_s[...]
    lane = lax.broadcasted_iota(jnp.int32, q.shape, 1) // HEAD_DIM
    for h in range(2):
        part = jnp.where(lane == h, q, jnp.zeros_like(q))
        qm[h] = part
        qtm[h] = part.T
    fk.step(1)
    fk.step(2)
    fv.offer(0)
    og.step(1)
    fk.step(3)
    og.step(2)
    loads[4].wait()
    og.step(3)

    def project(i, carry):
        rows = rows_at(i, QB)
        acc = None
        for g in range(2 * NX):
            part = lax.dot_general(
                og_all[g, rows, :],
                w_rows[:, pl.ds(g * COLS, COLS)],
                (((1,), (1,)), ((), ())),
                preferred_element_type=jnp.float32,
            )
            acc = part if acc is None else acc + part
        da = acc.astype(BF)
        half = lax.broadcasted_iota(jnp.int32, da.shape, 1) // HEAD_DIM
        for h in range(2):
            part = jnp.where(half == h, da, jnp.zeros_like(da))
            dam[h, rows, :] = part
            datm[h, :, rows] = part.T
        return carry

    lax.fori_loop(0, tokens // QB, project, 0)
    fk.step(4)
    fv.offer(1)
    fk.step(5)
    fv.step(1)
    fk.step(6)
    fv.step(2)
    fk.step(7)
    for j in range(slots):
        k_s[pl.ds(j * BLOCK, BLOCK), :] = got_k[pack[views, j]]

    tiles = tokens // QB
    turns = SCALE * LOG2E

    def score(h, cols, c, top):
        rows = pl.ds(c * KC, KC)
        s = dot(k_s[rows, :], qtm[h, :, cols])
        s_s[h, rows, :] = s
        return jnp.maximum(top, jnp.max(s, axis=0, keepdims=True))

    lowest = jnp.full((1, QB), -jnp.inf, F32)

    def tile(h, cols, top, other, other_cols):
        shift = top * turns
        total = jnp.zeros((1, QB), F32)
        other_top = lowest
        for c in range(chunks):
            other_top = score(other, other_cols, c, other_top)
            rows = pl.ds(c * KC, KC)
            e = jnp.exp2(s_s[h, rows, :] * turns - shift)
            p_s[h, rows, cols] = e.astype(BF)
            total = total + jnp.sum(e, axis=0, keepdims=True)
        inv = jnp.broadcast_to(1.0 / total, (8, QB))
        inv_s[h, :, cols] = inv
        down = inv.T[:, 0:1]
        dam[h, cols, :] = (dam[h, cols, :].astype(F32) * down).astype(BF)
        qm[h, cols, :] = (qm[h, cols, :].astype(F32) * down).astype(BF)
        return other_top

    def forward(i, top):
        cols = rows_at(i, QB)
        after = rows_at(jnp.minimum(i + 1, tiles - 1), QB)
        top = tile(0, cols, top, 1, cols)

        @pl.when(i == 1)
        def _():
            fv.step(3)

        return tile(1, cols, top, 0, after)

    top = lowest
    for c in range(chunks):
        top = score(0, pl.ds(0, QB), c, top)
    lax.fori_loop(0, tiles, forward, top)

    wide = 4 * BLOCK

    def grads(c, right):
        rows = rows_at(c, wide)
        g = dot(p_s[0, rows, :], right[0]) + dot(p_s[1, rows, :], right[1])
        g = g.astype(BF)
        for b in range(4):
            grad_s[c * 4 + b] = g[b * BLOCK : (b + 1) * BLOCK, :]

    def hand_out(sent, held, low, high):
        for e in range(low, high):
            held[0, e] = grad_s[pack[views + 8, e]]
            for k in range(1, NY):
                sent[k - 1, e] = grad_s[pack[views + 8, k * NZ + e]]

    def value_grads(c, carry):
        @pl.when(c == 1)
        def _():
            hand_out(sent_v, held_v, 7, 8)
            rv.start_y(0)

        @pl.when(c == 3)
        def _():
            hand_out(sent_v, held_v, 5, 7)
            rv.start_y(1)
            rv.step(0)

        grads(c, dam)
        return carry

    fv.step(4)
    fk.step(8)
    og.step(4)
    lax.fori_loop(0, keys // wide, value_grads, 0)
    fv.step(5)
    rv.step(1)
    fv.step(6)
    hand_out(sent_v, held_v, 0, 5)
    rv.start_y(2)
    rv.step(2)
    rv.step(3)
    rv.start_y(3)
    rv.start_y(4)
    for j in range(slots):
        kt_s[:, pl.ds(j * BLOCK, BLOCK)] = k_s[pl.ds(j * BLOCK, BLOCK), :].T
    fv.step(7)
    for j in range(slots):
        rows = pl.ds(j * BLOCK, BLOCK)
        block = got_v[pack[views, j]]
        v_s[rows, :] = block
        vt_s[:, rows] = block.T

    def attend(i, carry):
        @pl.when(i == 1)
        def _():
            rv.step(4)

        @pl.when(i == 2)
        def _():
            rv.step(5)

        cols = rows_at(i, QB)
        for h in range(2):
            band = pl.ds(h * HEAD_DIM, HEAD_DIM)
            att = dot(vt_s[band, :], p_s[h, :, cols]) * inv_s[h, 0:1, cols]
            att = att.astype(BF)
            att_t[band, cols] = att
            delta = jnp.sum(
                att.astype(F32) * datm[h, band, cols].astype(F32), axis=0, keepdims=True
            )
            delta_s[h, :, cols] = jnp.broadcast_to(delta, (8, QB))
        return carry

    lax.fori_loop(0, tiles, attend, 0)
    fv.step(8)
    att_s[...] = att_t[...].T
    at.step(0)

    def key_grads(c, carry):
        @pl.when(c == 1)
        def _():
            hand_out(sent_k, held_k, 7, 8)
            rk.start_y(0)

        @pl.when(c == 3)
        def _():
            hand_out(sent_k, held_k, 5, 7)
            rk.start_y(1)
            rv.step(6)
            rk.step(0)
            rk.step(1)

        rows = rows_at(c, wide)
        total, held = None, None
        for h in range(2):
            for i in range(tiles):
                cols = pl.ds(i * QB, QB)
                dp = dot(v_s[rows, :], datm[h, :, cols])
                if held is not None:
                    part = dot(*held)
                    total = part if total is None else total + part
                dp = dp - delta_s[h, 0:1, cols]
                ds = (p_s[h, rows, cols].astype(F32) * dp).astype(BF)
                p_s[h, rows, cols] = ds
                held = (ds, qm[h, cols, :])
        total = ((total + dot(*held)) * SCALE).astype(BF)
        for b in range(4):
            grad_s[c * 4 + b] = total[b * BLOCK : (b + 1) * BLOCK, :]
        return carry

    lax.fori_loop(0, keys // wide, key_grads, 0)
    hand_out(sent_k, held_k, 0, 5)
    rk.start_y(2)
    rk.start_y(3)
    rk.start_y(4)
    at.step(1)

    def query_grads(i, carry):
        @pl.when(i == 3)
        def _():
            rk.step(2)

        cols = rows_at(i, QB)
        for h in range(2):
            band = pl.ds(h * HEAD_DIM, HEAD_DIM)
            dq = dot(kt_s[band, :], p_s[h, :, cols]) * (inv_s[h, 0:1, cols] * SCALE)
            dq_t[band, cols] = dq.astype(BF)
        return carry

    lax.fori_loop(0, tiles, query_grads, 0)
    rk.step(3)
    rv.step(7)
    dq_ref[...] = dq_t[...].T
    stores[0].start()
    at.step(2)
    rk.step(4)
    rk.step(5)
    loads[5].wait()
    at.step(3)

    def mix(i, carry):
        rows = rows_at(i, QB)
        acc = None
        for g in range(2 * NX):
            part = dot(at_all[g, rows, :], w_cols[pl.ds(g * COLS, COLS), :])
            acc = part if acc is None else acc + part
        mixed_ref[rows, :] = acc.astype(BF)
        return carry

    lax.fori_loop(0, tokens // QB, mix, 0)
    stores[1].start()
    rk.step(6)
    rv.step(8)
    rv.step(9)
    stores[2].start()
    rk.step(7)
    at.step(4)
    rv.step(10)
    rk.step(8)
    stores[3].start()
    rk.step(9)
    stores[4].start()
    rk.step(10)
    for store in stores:
        store.wait()


def layer(sv, sb, q, k, v, w, og):
    tokens = q.shape[0]
    slots, views = sv.shape
    keys = slots * BLOCK
    hbm = pl.BlockSpec(memory_space=pl.ANY)
    vm = pl.BlockSpec(memory_space=pltpu.VMEM)

    def vmem(*shape, dtype=BF):
        return pltpu.VMEM(shape, dtype)

    def bufs(cls):
        return [vmem(b, a, BLOCK, COLS) for a, b in cls.scratch]

    rows = jax.ShapeDtypeStruct((tokens, COLS), BF)
    cut = jax.ShapeDtypeStruct((NB, BLOCK, COLS), BF)
    return pl.pallas_call(
        layer_kernel,
        out_shape=(rows, rows, cut, cut),
        in_specs=[vm, vm] + [hbm] * 5,
        out_specs=(hbm,) * 4,
        scratch_shapes=bufs(Fetch) + bufs(Fetch) + bufs(Return) + bufs(Return) + [
            vmem(NB, BLOCK, COLS),
            vmem(NB, BLOCK, COLS),
            vmem(tokens, COLS),
            vmem(tokens, COLS),
            vmem(COLS, w.shape[1]),
            vmem(w.shape[0], COLS),
            vmem(NY * NZ, BLOCK, COLS),
            vmem(NY * NZ, BLOCK, COLS),
            vmem(2 * NX, tokens, COLS),
            vmem(2 * NX, tokens, COLS),
            vmem(NY - 1, NZ, BLOCK, COLS),
            vmem(NY - 1, NZ, BLOCK, COLS),
            vmem(NY, NZ, BLOCK, COLS),
            vmem(NY, NZ, BLOCK, COLS),
            vmem(2, tokens, COLS),
            vmem(2, COLS, tokens),
            vmem(2, tokens, COLS),
            vmem(2, COLS, tokens),
            vmem(keys, COLS),
            vmem(COLS, keys),
            vmem(keys, COLS),
            vmem(COLS, keys),
            vmem(2, keys, QB, dtype=F32),
            vmem(2, keys, tokens),
            vmem(COLS, tokens),
            vmem(COLS, tokens),
            vmem(slots, BLOCK, COLS),
            vmem(tokens, COLS),
            vmem(tokens, COLS),
            vmem(tokens, COLS),
            vmem(NB, BLOCK, COLS),
            vmem(NB, BLOCK, COLS),
            vmem(2, 8, tokens, dtype=F32),
            vmem(2, 8, tokens, dtype=F32),
            vmem(views + 16, BLOCK, dtype=jnp.int32),
            pltpu.SMEM((views + 16, BLOCK), jnp.int32),
            pltpu.SemaphoreType.DMA((74,)),
            pltpu.SemaphoreType.DMA((74,)),
            pltpu.SemaphoreType.DMA((12,)),
        ],
        compiler_params=pltpu.CompilerParams(
            collective_id=0, has_side_effects=True, vmem_limit_bytes=56 * 2**20
        ),
        name="layer",
    )(sv, sb, q, k, v, w, og)


def finish_kernel(*refs):
    sems = refs[-1]
    n = (len(refs) - 1) // 2
    moves = [pltpu.make_async_copy(refs[i], refs[n + i], sems.at[i]) for i in range(n)]
    for move in moves:
        move.start()
    for move in moves:
        move.wait()


def finish(*arrays):
    vm = pl.BlockSpec(memory_space=pltpu.VMEM)
    hbm = pl.BlockSpec(memory_space=pl.ANY)
    return pl.pallas_call(
        finish_kernel,
        out_shape=tuple(jax.ShapeDtypeStruct(a.shape, a.dtype) for a in arrays),
        in_specs=[vm] * len(arrays),
        out_specs=(hbm,) * len(arrays),
        scratch_shapes=[pltpu.SemaphoreType.DMA((len(arrays),))],
        name="finish",
    )(*arrays)


def body(query_rows, key_rows, value_rows, out_weight, out_grad, source_view, source_block):
    cut = (NB, BLOCK, COLS)
    mixed, dq, kg, vg = finish(*layer(
        source_view.T, source_block.T,
        query_rows, key_rows.reshape(cut), value_rows.reshape(cut), out_weight, out_grad,
    ))
    return mixed, dq, kg.reshape(query_rows.shape), vg.reshape(query_rows.shape)


def solution(mesh):
    spread = P("view", "head")
    return jax.shard_map(
        body,
        mesh=mesh,
        in_specs=(spread, spread, spread, P(), spread, P(), P()),
        out_specs=(spread, spread, spread, spread),
        check_vma=False,
    )
```
